32 devices in a mesh: pair: 32 (over z, y, x, core), aux: 1.
Axes of the slice: x: 2, y: 2, z: 4, core: 2. Of those that a mesh axis runs over, the one named last changes fastest.
Arguments:
- amplitudes: bfloat16 [256, 512, 512], P(None, 'pair'), may hold values from -6 to 6
- ladder: bfloat16 [256, 256], replicated, may hold values from -0.375 to 0.375
- cholesky: bfloat16 [8, 512, 512], P('aux'), may hold values from -0.25 to 0.25
- pair_ids: int32 [256], P('pair'), may hold values from 0 to 255, each once
- occ_energy: float32 [16], replicated, may hold values from -2 to -0.5
- vir_energy: float32 [512], replicated, may hold values from 0.5 to 3
Outputs:
- update: float32 [256, 512, 512], P('pair', None, 'aux')
The draws below stay inside these ranges and needn't reach their ends.
Inputs may be any that keep to these rules, and one draw needn't show every extreme that they name: `pair_ids`: every value 0 to 255 appears once.
All inputs are finite; a program needn't handle non-finite values.
Results may differ from the reference program's by a relative error of at most 0.0029.
Values may be sent and summed in bfloat16 or wider, within the bound.
A program may use at most 128 MiB of HBM per device.

```python
import jax
import jax.numpy as jnp
from jax import lax

NO = 16
NV = 512
OP = 256
NQ = 8


def block_scale(key, shape, pieces, low, top_value):
    def one(dim, shards_of):
        draws = jax.random.uniform(jax.random.fold_in(jax.random.fold_in(key, 6), dim), (shards_of,), jnp.float32, low / len(pieces), top_value / len(pieces))
        return jnp.repeat(jnp.exp(draws), shape[dim] // shards_of).reshape((-1,) + (1,) * (len(shape) - dim - 1))

    level = one(*pieces[0])
    for cut in pieces[1:]:
        level = level * one(*cut)
    return level


def centred(rng, extent, spread, most, split=(), dtype=jnp.bfloat16):
    entries = spread * jax.random.normal(rng, extent, jnp.float32)
    if split:
        entries = entries * block_scale(rng, extent, split, -0.22, 0.18)
    return jnp.clip(entries, -most, most).astype(dtype)


def setup_inputs(seed: int = 0) -> dict:
    seeds = jax.random.split(jax.random.key(seed), 7)
    return {
        "amplitudes": centred(seeds[0], (OP, NV, NV), 1.0, 6.0, ((1, 32),)),
        "ladder": centred(seeds[1], (OP, OP), OP ** -0.5, 0.375),
        "cholesky": centred(seeds[2], (NQ, NV, NV), NV ** -0.5, 0.25),
        "pair_ids": jax.random.permutation(seeds[3], OP).astype(jnp.int32),
        "occ_energy": jnp.clip(jax.random.uniform(seeds[4], (NO,), jnp.float32, -2.0, -0.5), -2.0, -0.5),
        "vir_energy": jnp.clip(jax.random.uniform(seeds[5], (NV,), jnp.float32, 0.5, 3.0), 0.5, 3.0),
    }


def reference(amplitudes, ladder, cholesky, pair_ids, occ_energy, vir_energy):
    flat_amps = amplitudes.reshape(OP, NV * NV)
    hole_term = jnp.dot(ladder, flat_amps, preferred_element_type=jnp.float32).astype(jnp.bfloat16)
    hole_term = hole_term.reshape(OP, NV, NV)
    by_first = jnp.transpose(amplitudes, (1, 0, 2)).reshape(NV, OP * NV)

    def add_vector(running, vector):
        mixed_terms = jnp.dot(vector, by_first, preferred_element_type=jnp.float32).astype(jnp.bfloat16)
        mixed_terms = jnp.transpose(mixed_terms.reshape(NV, OP, NV), (1, 0, 2)).reshape(OP * NV, NV)
        product = jnp.dot(mixed_terms, vector.T, preferred_element_type=jnp.float32)
        return running + product.reshape(OP, NV, NV), None

    particle, _ = lax.scan(add_vector, jnp.zeros((OP, NV, NV), jnp.float32), cholesky)
    first_occ = (pair_ids // NO).astype(jnp.int32)
    second_occ = (pair_ids % NO).astype(jnp.int32)
    occ_sum = occ_energy[first_occ] + occ_energy[second_occ]
    denominator = vir_energy[None, :, None] + vir_energy[None, None, :] - occ_sum[:, None, None]
    return (hole_term.astype(jnp.float32) + particle) / denominator
```

```python
import functools

import jax
import jax.numpy as jnp
from jax import lax
from jax.experimental import pallas as pl
from jax.experimental.pallas import tpu as pltpu
from jax.sharding import PartitionSpec as P

NO = 16
VMEM_BYTES = 67043328
MESH = pl.DeviceIdType.MESH


def by_core(core, even, odd):
    return even + core * (odd - even)


def send_orders(n):
    half, quarter = n // 2, n // 4
    crossing = [a + b for a in range(quarter) for b in (half + quarter, half)]
    staying = [a + b for a in range(quarter) for b in (quarter, 0) if a + b]
    return crossing, staying


def arrival_order(first, second):
    return [k for k in first if k % 2 == 0] + [k for k in second if k % 2], [k for k in second if k % 2 == 0] + [k for k in first if k % 2]


def residual_kernel(
    n, amps, ladder, chol, pair_ids, occ, vir, result, own_hole,
    amp_own, wide, ladder_v, chol_v, amp_all, hole_all, vir_sum, vir_v, ids_s, occ_s,
    amp_send, amp_recv, hole_send, hole_recv, local_sem,
):
    total, rows, width = amps.shape
    pairs = total // n
    full = rows * n
    n_vec = chol.shape[0]
    me = lax.axis_index("pair")
    core = me % 2
    crossing, staying = send_orders(n)
    mine = pl.ds(pl.multiple_of(me * rows, rows), rows)
    own_pairs = pl.ds(me * pairs, pairs)

    def rows_of(source):
        return pl.ds(pl.multiple_of(source * rows, rows), rows)

    def amp_copy(k):
        dest = me ^ k
        return pltpu.make_async_remote_copy(
            amps.at[pl.ds(dest * pairs, pairs)], amp_all.at[:, mine],
            amp_send.at[k], amp_recv.at[k], device_id={"pair": dest}, device_id_type=MESH,
        )

    def hole_copy(k):
        dest = me ^ k
        return pltpu.make_async_remote_copy(
            own_hole.at[pl.ds(dest * pairs, pairs)], hole_all.at[:, mine],
            hole_send.at[k], hole_recv.at[k], device_id={"pair": dest}, device_id_type=MESH,
        )

    load_amp = pltpu.make_async_copy(amps, amp_own, local_sem.at[0])
    load_ladder = pltpu.make_async_copy(ladder, ladder_v, local_sem.at[1])
    load_chol = pltpu.make_async_copy(chol, chol_v, local_sem.at[2])
    keep_amp = pltpu.make_async_copy(amps.at[own_pairs], amp_all.at[:, mine], local_sem.at[3])
    load_ids = pltpu.make_async_copy(pair_ids, ids_s, local_sem.at[4])
    load_occ = pltpu.make_async_copy(occ, occ_s, local_sem.at[5])
    load_vir = pltpu.make_async_copy(vir, vir_v, local_sem.at[6])

    barrier = pltpu.get_barrier_semaphore()
    for k in range(1, n):
        pl.semaphore_signal(barrier, inc=1, device_id={"pair": me ^ k}, device_id_type=MESH)
    pl.semaphore_wait(barrier, n - 1)

    for even, odd in zip(crossing + staying, staying + crossing):
        amp_copy(by_core(core, even, odd)).start()
    load_amp.start()
    load_ladder.start()
    load_chol.start()
    keep_amp.start()
    load_ids.start()
    load_occ.start()
    load_vir.start()

    load_amp.wait()
    load_ladder.wait()
    block = 16
    lanes = 128

    def columns(j, carry):
        cols = pl.ds(pl.multiple_of(j * lanes, lanes), lanes)

        def widen(i, c):
            part = amp_own[pl.ds(i * block, block), :, cols].astype(jnp.float32)
            wide[pl.ds(pl.multiple_of(i * block * rows, block * rows), block * rows), :] = part.reshape(block * rows, lanes)
            return c

        lax.fori_loop(0, total // block, widen, 0)

        def one_row(a, c):
            sel = pl.ds(a, total, stride=rows)
            value = wide[sel, :].astype(jnp.bfloat16)
            wide[sel, :] = jnp.dot(ladder_v[...], value, preferred_element_type=jnp.float32)
            return c

        lax.fori_loop(0, rows, one_row, 0)

        def narrow(i, c):
            part = wide[pl.ds(pl.multiple_of(i * block * rows, block * rows), block * rows), :].astype(jnp.bfloat16)
            amp_own[pl.ds(i * block, block), :, cols] = part.reshape(block, rows, lanes)
            return c

        lax.fori_loop(0, total // block, narrow, 0)
        return carry

    lax.fori_loop(0, width // lanes, columns, 0)
    store_hole = pltpu.make_async_copy(amp_own, own_hole, local_sem.at[0])
    store_hole.start()
    store_hole.wait()

    for even, odd in zip(staying + crossing, crossing + staying):
        hole_copy(by_core(core, even, odd)).start()
    keep_hole = pltpu.make_async_copy(own_hole.at[own_pairs], hole_all.at[:, mine], local_sem.at[1])
    keep_hole.start()

    load_ids.wait()
    load_occ.wait()
    load_vir.wait()

    def add_virtuals(i, carry):
        at = pl.ds(pl.multiple_of(i * lanes, lanes), lanes)
        row = vir_v[:, at]
        diagonal = lax.broadcasted_iota(jnp.int32, (lanes, lanes), 0) == lax.broadcasted_iota(jnp.int32, (lanes, lanes), 1)
        column = jnp.sum(jnp.where(diagonal, row, 0.0), axis=1, keepdims=True)
        vir_sum[at, :] = column + vir_v[...]
        return carry

    lax.fori_loop(0, full // lanes, add_virtuals, 0)

    load_chol.wait()
    keep_amp.wait()
    for k in range(1, n):
        amp_copy(k).wait_recv()

    def one_pair(p, carry):
        result[p] = jnp.zeros((full, full), jnp.float32)

        def one_vector(q, c):
            vector = chol_v[q]
            mixed = jnp.dot(vector, amp_all[p], preferred_element_type=jnp.float32).astype(jnp.bfloat16)
            result[p] += lax.dot_general(
                mixed, vector, (((1,), (1,)), ((), ())), preferred_element_type=jnp.float32
            )
            return c

        lax.fori_loop(0, n_vec, one_vector, 0)
        return carry

    lax.fori_loop(0, pairs, one_pair, 0)

    def finish(k):
        at = rows_of(me ^ k)

        def one(p, carry):
            pair = ids_s[p]
            shift = occ_s[pair // NO] + occ_s[pair % NO]
            value = hole_all[p, at, :].astype(jnp.float32) + result[p, at, :]
            result[p, at, :] = value / (vir_sum[at, :] - shift)
            return carry

        lax.fori_loop(0, pairs, one, 0)

    keep_hole.wait()
    finish(0)
    early, late = arrival_order(staying, crossing)
    for even, odd in zip(early + late, late + early):
        k = by_core(core, even, odd)
        hole_copy(k).wait_recv()
        finish(k)
    for k in range(1, n):
        amp_copy(k).wait_send()
        hole_copy(k).wait_send()


def write_kernel(result, out, sems):
    pieces = sems.shape[0]
    size = result.shape[0] // pieces
    puts = [
        pltpu.make_async_copy(result.at[pl.ds(i * size, size)], out.at[pl.ds(i * size, size)], sems.at[i])
        for i in range(pieces)
    ]
    for put in puts:
        put.start()
    for put in puts:
        put.wait()


def exchange_and_contract(amplitudes, ladder, cholesky, pair_ids, occ_energy, vir_energy):
    n = lax.axis_size("pair")
    total, rows, width = amplitudes.shape
    pairs = total // n
    full = rows * n
    anywhere = pl.BlockSpec(memory_space=pl.ANY)
    in_hbm = pl.BlockSpec(memory_space=pltpu.HBM)
    in_vmem = pl.BlockSpec(memory_space=pltpu.VMEM)
    result, _ = pl.pallas_call(
        functools.partial(residual_kernel, n),
        out_shape=[
            pltpu.VMEM((pairs, full, full), jnp.float32),
            jax.ShapeDtypeStruct(amplitudes.shape, jnp.bfloat16),
        ],
        in_specs=[in_hbm] * 6,
        out_specs=[in_vmem, in_hbm],
        scratch_shapes=[
            pltpu.VMEM(amplitudes.shape, jnp.bfloat16),
            pltpu.VMEM((total * rows, 128), jnp.float32),
            pltpu.VMEM(ladder.shape, jnp.bfloat16),
            pltpu.VMEM(cholesky.shape, jnp.bfloat16),
            pltpu.VMEM((pairs, full, width), jnp.bfloat16),
            pltpu.VMEM((pairs, full, width), jnp.bfloat16),
            pltpu.VMEM((full, full), jnp.float32),
            pltpu.VMEM((1, full), jnp.float32),
            pltpu.SMEM(pair_ids.shape, jnp.int32),
            pltpu.SMEM(occ_energy.shape, jnp.float32),
            pltpu.SemaphoreType.DMA((n,)),
            pltpu.SemaphoreType.DMA((n,)),
            pltpu.SemaphoreType.DMA((n,)),
            pltpu.SemaphoreType.DMA((n,)),
            pltpu.SemaphoreType.DMA((7,)),
        ],
        compiler_params=pltpu.CompilerParams(
            collective_id=0, has_side_effects=True, vmem_limit_bytes=VMEM_BYTES - 4 * pairs * full * full
        ),
    )(amplitudes, ladder, cholesky, pair_ids, occ_energy, vir_energy.reshape(1, -1))
    return pl.pallas_call(
        write_kernel,
        out_shape=jax.ShapeDtypeStruct((pairs, full, full), jnp.float32),
        in_specs=[in_vmem],
        out_specs=in_hbm,
        scratch_shapes=[pltpu.SemaphoreType.DMA((pairs,))],
        compiler_params=pltpu.CompilerParams(vmem_limit_bytes=8 * 1024 * 1024),
    )(result)


def exchange_plain(amplitudes, ladder, cholesky):
    flat = amplitudes.reshape(amplitudes.shape[0], -1)
    hole = jnp.dot(ladder, flat, preferred_element_type=jnp.float32).astype(jnp.bfloat16)
    hole = hole.reshape(amplitudes.shape)
    pair_amps = lax.all_to_all(amplitudes, "pair", split_axis=0, concat_axis=1, tiled=True)
    pair_hole = lax.all_to_all(hole, "pair", split_axis=0, concat_axis=1, tiled=True)
    mixed = jnp.einsum(
        "qac,pcd->qpad", cholesky, pair_amps, preferred_element_type=jnp.float32
    ).astype(jnp.bfloat16)
    particle = jnp.einsum("qpad,qbd->pab", mixed, cholesky, preferred_element_type=jnp.float32)
    return pair_hole, particle


def shards(amplitudes, ladder, cholesky, pair_ids, occ_energy, vir_energy):
    n = lax.axis_size("pair")
    n_aux = lax.axis_size("aux")
    half_width = amplitudes.shape[2] // n_aux
    aux_index = lax.axis_index("aux")
    aligned = amplitudes.shape[1] % 16 == 0 and n & (n - 1) == 0 and n >= 4
    if aligned and n_aux == 1:
        return exchange_and_contract(amplitudes, ladder, cholesky, pair_ids, occ_energy, vir_energy)
    hole, particle = exchange_plain(amplitudes, ladder, cholesky)
    if n_aux > 1:
        hole = lax.dynamic_slice_in_dim(hole, aux_index * half_width, half_width, 2)
        particle = lax.psum_scatter(particle, "aux", scatter_dimension=2, tiled=True)
    orbitals = jnp.arange(NO, dtype=jnp.int32)
    first_hot = (pair_ids // NO)[:, None] == orbitals[None, :]
    second_hot = (pair_ids % NO)[:, None] == orbitals[None, :]
    hot = first_hot.astype(jnp.float32) + second_hot.astype(jnp.float32)
    occ_sum = jnp.sum(hot * occ_energy[None, :], axis=1)
    vir_cols = lax.dynamic_slice_in_dim(vir_energy, aux_index * half_width, half_width, 0)
    denominator = vir_energy[None, :, None] + vir_cols[None, None, :] - occ_sum[:, None, None]
    return (hole.astype(jnp.float32) + particle) / denominator


def solution(mesh):
    in_specs = (P(None, "pair", None), P(), P("aux", None, None), P("pair"), P(), P())
    out_specs = P("pair", None, "aux")
    return jax.shard_map(shards, mesh=mesh, in_specs=in_specs, out_specs=out_specs, check_vma=False)
```

```python
import functools

import jax
import jax.numpy as jnp
from jax import lax
from jax.experimental import pallas as pl
from jax.experimental.pallas import tpu as pltpu
from jax.sharding import PartitionSpec as P

NO = 16
VMEM_BYTES = 67043328
LAST = 4
STEP = 4
MESH = pl.DeviceIdType.MESH


def by_core(core, even, odd):
    return even + core * (odd - even)


def send_orders(n):
    half, quarter = n // 2, n // 4
    crossing = [a + b for a in range(quarter) for b in (half + quarter, half)]
    staying = [a + b for a in range(quarter) for b in (quarter, 0) if a + b]
    return crossing, staying


def arrival_orders(crossing, staying):
    cross = [k for k in crossing if k % 2 == 0], [k for k in crossing if k % 2]
    stay = [k for k in staying if k % 2 == 0], [k for k in staying if k % 2]
    amps = cross[0] + stay[1] + stay[0] + cross[1], stay[0] + cross[1] + stay[1] + cross[0]
    holes = stay[0] + cross[1] + stay[1] + cross[0], stay[1] + cross[0] + stay[0] + cross[1]
    return amps, holes


def residual_kernel(
    n, amps, ladder, chol, pair_ids, occ, vir, result, own_hole,
    amp_own, wide, ladder_v, chol_v, amp_all, hole_all, inverse, vir_v, ids_s, occ_s,
    amp_send, amp_recv, hole_send, hole_recv, local_sem,
):
    total, rows, width = amps.shape
    pairs = total // n
    full = rows * n
    n_vec = chol.shape[0]
    me = lax.axis_index("pair")
    core = me % 2
    crossing, staying = send_orders(n)
    mine = pl.ds(pl.multiple_of(me * rows, rows), rows)
    own_pairs = pl.ds(me * pairs, pairs)

    def rows_of(source):
        return pl.ds(pl.multiple_of(source * rows, rows), rows)

    def amp_copy(k):
        dest = me ^ k
        return pltpu.make_async_remote_copy(
            amps.at[pl.ds(dest * pairs, pairs)], amp_all.at[:, mine],
            amp_send.at[k], amp_recv.at[k], device_id={"pair": dest}, device_id_type=MESH,
        )

    def hole_copy(k):
        dest = me ^ k
        return pltpu.make_async_remote_copy(
            own_hole.at[pl.ds(dest * pairs, pairs)], hole_all.at[:, mine],
            hole_send.at[k], hole_recv.at[k], device_id={"pair": dest}, device_id_type=MESH,
        )

    load_amp = pltpu.make_async_copy(amps, amp_own, local_sem.at[0])
    load_ladder = pltpu.make_async_copy(ladder, ladder_v, local_sem.at[1])
    load_chol = pltpu.make_async_copy(chol, chol_v, local_sem.at[2])
    keep_amp = pltpu.make_async_copy(amps.at[own_pairs], amp_all.at[:, mine], local_sem.at[3])
    load_ids = pltpu.make_async_copy(pair_ids, ids_s, local_sem.at[4])
    load_occ = pltpu.make_async_copy(occ, occ_s, local_sem.at[5])
    load_vir = pltpu.make_async_copy(vir, vir_v, local_sem.at[6])

    barrier = pltpu.get_barrier_semaphore()
    for k in range(1, n):
        pl.semaphore_signal(barrier, inc=1, device_id={"pair": me ^ k}, device_id_type=MESH)
    pl.semaphore_wait(barrier, n - 1)

    for even, odd in zip(crossing + staying, staying + crossing):
        amp_copy(by_core(core, even, odd)).start()
    load_amp.start()
    load_ladder.start()
    load_chol.start()
    keep_amp.start()
    load_ids.start()
    load_occ.start()
    load_vir.start()

    load_amp.wait()
    load_ladder.wait()
    block = 16
    lanes = 128

    def columns(j, carry):
        cols = pl.ds(pl.multiple_of(j * lanes, lanes), lanes)

        def widen(i, c):
            part = amp_own[pl.ds(i * block, block), :, cols].astype(jnp.float32)
            wide[pl.ds(pl.multiple_of(i * block * rows, block * rows), block * rows), :] = part.reshape(block * rows, lanes)
            return c

        lax.fori_loop(0, total // block, widen, 0)

        def one_row(a, c):
            sel = pl.ds(a, total, stride=rows)
            value = wide[sel, :].astype(jnp.bfloat16)
            wide[sel, :] = jnp.dot(ladder_v[...], value, preferred_element_type=jnp.float32)
            return c

        lax.fori_loop(0, rows, one_row, 0)

        def narrow(i, c):
            part = wide[pl.ds(pl.multiple_of(i * block * rows, block * rows), block * rows), :].astype(jnp.bfloat16)
            amp_own[pl.ds(i * block, block), :, cols] = part.reshape(block, rows, lanes)
            return c

        lax.fori_loop(0, total // block, narrow, 0)
        return carry

    lax.fori_loop(0, width // lanes, columns, 0)
    store_hole = pltpu.make_async_copy(amp_own, own_hole, local_sem.at[0])
    store_hole.start()
    store_hole.wait()

    load_ids.wait()
    load_occ.wait()
    load_vir.wait()

    def one_inverse(p, carry):
        pair = ids_s[p]
        shift = occ_s[pair // NO] + occ_s[pair % NO]

        def add_virtuals(i, c):
            at = pl.ds(pl.multiple_of(i * lanes, lanes), lanes)
            row = vir_v[:, at]
            diagonal = lax.broadcasted_iota(jnp.int32, (lanes, lanes), 0) == lax.broadcasted_iota(jnp.int32, (lanes, lanes), 1)
            column = jnp.sum(jnp.where(diagonal, row, 0.0), axis=1, keepdims=True)
            inverse[p, at, :] = 1.0 / (column + vir_v[...] - shift)
            return c

        lax.fori_loop(0, full // lanes, add_virtuals, 0)
        return carry

    lax.fori_loop(0, pairs, one_inverse, 0)

    amp_order, hole_order = arrival_orders(crossing, staying)
    arrived = [by_core(core, even, odd) for even, odd in zip(*amp_order)]
    sent = [by_core(core, even, odd) for even, odd in zip(staying + crossing, crossing + staying)]
    for k in sent[:len(staying)]:
        amp_copy(k).wait_send()
        hole_copy(k).start()
    for k in arrived[:-LAST]:
        amp_copy(k).wait_recv()
    for i, k in enumerate(sent[len(staying):]):
        amp_copy(k).wait_send()
        hole_copy(k).start()
        if STEP <= i + 1 < STEP + LAST:
            amp_copy(arrived[i + 1 - STEP - LAST]).wait_recv()
    keep_hole = pltpu.make_async_copy(own_hole.at[own_pairs], hole_all.at[:, mine], local_sem.at[1])
    keep_hole.start()

    load_chol.wait()
    keep_amp.wait()

    def one_pair(p, carry):
        result[p] = jnp.zeros((full, full), jnp.float32)

        def one_vector(q, c):
            vector = chol_v[q]
            mixed = jnp.dot(vector, amp_all[p], preferred_element_type=jnp.float32).astype(jnp.bfloat16)
            result[p] += lax.dot_general(
                mixed, vector, (((1,), (1,)), ((), ())), preferred_element_type=jnp.float32
            )
            return c

        lax.fori_loop(0, n_vec, one_vector, 0)
        return carry

    lax.fori_loop(0, pairs, one_pair, 0)

    def finish(k):
        at = rows_of(me ^ k)

        def one(p, carry):
            result[p, at, :] = (hole_all[p, at, :].astype(jnp.float32) + result[p, at, :]) * inverse[p, at, :]
            return carry

        lax.fori_loop(0, pairs, one, 0)

    keep_hole.wait()
    finish(0)
    for even, odd in zip(*hole_order):
        k = by_core(core, even, odd)
        hole_copy(k).wait_recv()
        finish(k)
    for k in range(1, n):
        hole_copy(k).wait_send()


def write_kernel(result, out, sems):
    pieces = sems.shape[0]
    size = result.shape[0] // pieces
    puts = [
        pltpu.make_async_copy(result.at[pl.ds(i * size, size)], out.at[pl.ds(i * size, size)], sems.at[i])
        for i in range(pieces)
    ]
    for put in puts:
        put.start()
    for put in puts:
        put.wait()


def exchange_and_contract(amplitudes, ladder, cholesky, pair_ids, occ_energy, vir_energy):
    n = lax.axis_size("pair")
    total, rows, width = amplitudes.shape
    pairs = total // n
    full = rows * n
    anywhere = pl.BlockSpec(memory_space=pl.ANY)
    in_hbm = pl.BlockSpec(memory_space=pltpu.HBM)
    in_vmem = pl.BlockSpec(memory_space=pltpu.VMEM)
    result, _ = pl.pallas_call(
        functools.partial(residual_kernel, n),
        out_shape=[
            pltpu.VMEM((pairs, full, full), jnp.float32),
            jax.ShapeDtypeStruct(amplitudes.shape, jnp.bfloat16),
        ],
        in_specs=[in_hbm] * 6,
        out_specs=[in_vmem, in_hbm],
        scratch_shapes=[
            pltpu.VMEM(amplitudes.shape, jnp.bfloat16),
            pltpu.VMEM((total * rows, 128), jnp.float32),
            pltpu.VMEM(ladder.shape, jnp.bfloat16),
            pltpu.VMEM(cholesky.shape, jnp.bfloat16),
            pltpu.VMEM((pairs, full, width), jnp.bfloat16),
            pltpu.VMEM((pairs, full, width), jnp.bfloat16),
            pltpu.VMEM((pairs, full, full), jnp.float32),
            pltpu.VMEM((1, full), jnp.float32),
            pltpu.SMEM(pair_ids.shape, jnp.int32),
            pltpu.SMEM(occ_energy.shape, jnp.float32),
            pltpu.SemaphoreType.DMA((n,)),
            pltpu.SemaphoreType.DMA((n,)),
            pltpu.SemaphoreType.DMA((n,)),
            pltpu.SemaphoreType.DMA((n,)),
            pltpu.SemaphoreType.DMA((7,)),
        ],
        compiler_params=pltpu.CompilerParams(
            collective_id=0, has_side_effects=True, vmem_limit_bytes=VMEM_BYTES - 4 * pairs * full * full
        ),
    )(amplitudes, ladder, cholesky, pair_ids, occ_energy, vir_energy.reshape(1, -1))
    return pl.pallas_call(
        write_kernel,
        out_shape=jax.ShapeDtypeStruct((pairs, full, full), jnp.float32),
        in_specs=[in_vmem],
        out_specs=in_hbm,
        scratch_shapes=[pltpu.SemaphoreType.DMA((pairs,))],
        compiler_params=pltpu.CompilerParams(vmem_limit_bytes=8 * 1024 * 1024),
    )(result)


def exchange_plain(amplitudes, ladder, cholesky):
    flat = amplitudes.reshape(amplitudes.shape[0], -1)
    hole = jnp.dot(ladder, flat, preferred_element_type=jnp.float32).astype(jnp.bfloat16)
    hole = hole.reshape(amplitudes.shape)
    pair_amps = lax.all_to_all(amplitudes, "pair", split_axis=0, concat_axis=1, tiled=True)
    pair_hole = lax.all_to_all(hole, "pair", split_axis=0, concat_axis=1, tiled=True)
    mixed = jnp.einsum(
        "qac,pcd->qpad", cholesky, pair_amps, preferred_element_type=jnp.float32
    ).astype(jnp.bfloat16)
    particle = jnp.einsum("qpad,qbd->pab", mixed, cholesky, preferred_element_type=jnp.float32)
    return pair_hole, particle


def shards(amplitudes, ladder, cholesky, pair_ids, occ_energy, vir_energy):
    n = lax.axis_size("pair")
    n_aux = lax.axis_size("aux")
    half_width = amplitudes.shape[2] // n_aux
    aux_index = lax.axis_index("aux")
    aligned = amplitudes.shape[1] % 16 == 0 and n & (n - 1) == 0 and n >= 4
    if aligned and n_aux == 1:
        return exchange_and_contract(amplitudes, ladder, cholesky, pair_ids, occ_energy, vir_energy)
    hole, particle = exchange_plain(amplitudes, ladder, cholesky)
    if n_aux > 1:
        hole = lax.dynamic_slice_in_dim(hole, aux_index * half_width, half_width, 2)
        particle = lax.psum_scatter(particle, "aux", scatter_dimension=2, tiled=True)
    orbitals = jnp.arange(NO, dtype=jnp.int32)
    first_hot = (pair_ids // NO)[:, None] == orbitals[None, :]
    second_hot = (pair_ids % NO)[:, None] == orbitals[None, :]
    hot = first_hot.astype(jnp.float32) + second_hot.astype(jnp.float32)
    occ_sum = jnp.sum(hot * occ_energy[None, :], axis=1)
    vir_cols = lax.dynamic_slice_in_dim(vir_energy, aux_index * half_width, half_width, 0)
    denominator = vir_energy[None, :, None] + vir_cols[None, None, :] - occ_sum[:, None, None]
    return (hole.astype(jnp.float32) + particle) / denominator


def solution(mesh):
    in_specs = (P(None, "pair", None), P(), P("aux", None, None), P("pair"), P(), P())
    out_specs = P("pair", None, "aux")
    return jax.shard_map(shards, mesh=mesh, in_specs=in_specs, out_specs=out_specs, check_vma=False)
```

```python
import functools

import jax
import jax.numpy as jnp
from jax import lax
from jax.experimental import pallas as pl
from jax.experimental.pallas import tpu as pltpu
from jax.sharding import PartitionSpec as P

NO = 16
VMEM_BYTES = 67043328
LAST = 4
STEP = 4
MESH = pl.DeviceIdType.MESH


def by_core(core, even, odd):
    return even + core * (odd - even)


def send_orders(n, mid):
    half, quarter = n // 2, n // 4
    near = [half + quarter * mid + a for a in range(quarter)]
    far = [half + quarter * (1 - mid) + a for a in range(quarter)]
    lead = quarter // 4
    mixed = [k for pair in zip(far, near[lead:]) for k in pair]
    outward = near[:lead] + mixed + far[quarter - lead:]
    mixed = [k for pair in zip(near, far[lead:]) for k in pair]
    inward = far[:lead] + mixed + near[quarter - lead:]
    staying = [a + b for a in range(quarter) for b in (quarter, 0) if a + b]
    return outward, inward, staying


def arrival_orders(n, staying):
    half, quarter = n // 2, n // 4
    crossing = [a + b for a in range(quarter) for b in (half + quarter, half)]
    cross = [k for k in crossing if k % 2 == 0], [k for k in crossing if k % 2]
    stay = [k for k in staying if k % 2 == 0], [k for k in staying if k % 2]
    amps = cross[0] + stay[1] + stay[0] + cross[1], stay[0] + cross[1] + stay[1] + cross[0]
    holes = stay[0] + cross[1] + stay[1] + cross[0], stay[1] + cross[0] + stay[0] + cross[1]
    return amps, holes


def residual_kernel(
    n, amps, ladder, chol, pair_ids, occ, vir, result, own_hole,
    amp_own, wide, ladder_v, chol_v, amp_all, hole_all, inverse, vir_v, ids_s, occ_s,
    amp_send, amp_recv, hole_send, hole_recv, local_sem, entry_sem,
):
    total, rows, width = amps.shape
    pairs = total // n
    full = rows * n
    n_vec = chol.shape[0]
    me = lax.axis_index("pair")
    core = me % 2
    half, quarter = n // 2, n // 4
    mid = (me // quarter + 1) // 2 % 2
    outward, inward, staying = send_orders(n, mid)
    mine = pl.ds(pl.multiple_of(me * rows, rows), rows)
    own_pairs = pl.ds(me * pairs, pairs)

    def rows_of(source):
        return pl.ds(pl.multiple_of(source * rows, rows), rows)

    def amp_copy(k):
        dest = me ^ k
        return pltpu.make_async_remote_copy(
            amps.at[pl.ds(dest * pairs, pairs)], amp_all.at[:, mine],
            amp_send.at[k], amp_recv.at[k], device_id={"pair": dest}, device_id_type=MESH,
        )

    def hole_copy(k):
        dest = me ^ k
        return pltpu.make_async_remote_copy(
            own_hole.at[pl.ds(dest * pairs, pairs)], hole_all.at[:, mine],
            hole_send.at[k], hole_recv.at[k], device_id={"pair": dest}, device_id_type=MESH,
        )

    load_amp = pltpu.make_async_copy(amps, amp_own, local_sem.at[0])
    load_ladder = pltpu.make_async_copy(ladder, ladder_v, local_sem.at[1])
    load_chol = pltpu.make_async_copy(chol, chol_v, local_sem.at[2])
    keep_amp = pltpu.make_async_copy(amps.at[own_pairs], amp_all.at[:, mine], local_sem.at[3])
    load_ids = pltpu.make_async_copy(pair_ids, ids_s, local_sem.at[4])
    load_occ = pltpu.make_async_copy(occ, occ_s, local_sem.at[5])
    load_vir = pltpu.make_async_copy(vir, vir_v, local_sem.at[6])

    def tell(sem, k):
        pl.semaphore_signal(sem, inc=1, device_id={"pair": me ^ k}, device_id_type=MESH)

    barrier = pltpu.get_barrier_semaphore()
    low_bits = [1 << i for i in range(quarter.bit_length() - 1)]
    across, along, last = range(len(low_bits), len(low_bits) + 3)

    @pl.when(mid == 1)
    def _():
        tell(barrier, half + quarter)

    for k in low_bits:
        tell(barrier, k)

    @pl.when(mid == 1)
    def _():
        tell(barrier, quarter)

    load_amp.start()
    load_ladder.start()
    load_chol.start()
    keep_amp.start()
    load_ids.start()
    load_occ.start()
    load_vir.start()

    pl.semaphore_wait(barrier, len(low_bits) + 1)

    def start_near(first, last):
        @pl.when(mid == 1)
        def _():
            for a in range(first, last):
                amp_copy(half + quarter + a).start()

    start_near(0, 1)
    for i, k in enumerate(low_bits):
        tell(entry_sem.at[i], k)
        pl.semaphore_wait(entry_sem.at[i], 1)
        start_near(k, 2 * k)

    @pl.when(mid == 1)
    def _():
        tell(entry_sem.at[across], half + quarter)
        pl.semaphore_wait(entry_sem.at[across], 2)
        tell(entry_sem.at[along], half + quarter)
        tell(entry_sem.at[along], quarter)
        pl.semaphore_wait(entry_sem.at[along], 1)
        tell(entry_sem.at[last], quarter)

    @pl.when(mid == 0)
    def _():
        tell(entry_sem.at[across], quarter)
        pl.semaphore_wait(entry_sem.at[along], 1)
        pl.semaphore_wait(entry_sem.at[last], 1)

    first = [by_core(core, even, odd) for even, odd in zip(outward + staying, staying + outward)]

    @pl.when(mid == 1)
    def _():
        for k in [half + a for a in range(quarter)] + staying:
            amp_copy(k).start()

    @pl.when(mid == 0)
    def _():
        for k in first:
            amp_copy(k).start()

    load_amp.wait()
    load_ladder.wait()
    block = 16
    lanes = 128

    def columns(j, carry):
        cols = pl.ds(pl.multiple_of(j * lanes, lanes), lanes)

        def widen(i, c):
            part = amp_own[pl.ds(i * block, block), :, cols].astype(jnp.float32)
            wide[pl.ds(pl.multiple_of(i * block * rows, block * rows), block * rows), :] = part.reshape(block * rows, lanes)
            return c

        lax.fori_loop(0, total // block, widen, 0)

        def one_row(a, c):
            sel = pl.ds(a, total, stride=rows)
            value = wide[sel, :].astype(jnp.bfloat16)
            wide[sel, :] = jnp.dot(ladder_v[...], value, preferred_element_type=jnp.float32)
            return c

        lax.fori_loop(0, rows, one_row, 0)

        def narrow(i, c):
            part = wide[pl.ds(pl.multiple_of(i * block * rows, block * rows), block * rows), :].astype(jnp.bfloat16)
            amp_own[pl.ds(i * block, block), :, cols] = part.reshape(block, rows, lanes)
            return c

        lax.fori_loop(0, total // block, narrow, 0)
        return carry

    lax.fori_loop(0, width // lanes, columns, 0)
    store_hole = pltpu.make_async_copy(amp_own, own_hole, local_sem.at[0])
    store_hole.start()
    store_hole.wait()

    load_ids.wait()
    load_occ.wait()
    load_vir.wait()

    def one_inverse(p, carry):
        pair = ids_s[p]
        shift = occ_s[pair // NO] + occ_s[pair % NO]

        def add_virtuals(i, c):
            at = pl.ds(pl.multiple_of(i * lanes, lanes), lanes)
            row = vir_v[:, at]
            diagonal = lax.broadcasted_iota(jnp.int32, (lanes, lanes), 0) == lax.broadcasted_iota(jnp.int32, (lanes, lanes), 1)
            column = jnp.sum(jnp.where(diagonal, row, 0.0), axis=1, keepdims=True)
            inverse[p, at, :] = 1.0 / (column + vir_v[...] - shift)
            return c

        lax.fori_loop(0, full // lanes, add_virtuals, 0)
        return carry

    lax.fori_loop(0, pairs, one_inverse, 0)

    amp_order, hole_order = arrival_orders(n, staying)
    arrived = [by_core(core, even, odd) for even, odd in zip(*amp_order)]
    sent = [by_core(core, even, odd) for even, odd in zip(staying + inward, inward + staying)]
    for k in sent[:len(staying)]:
        amp_copy(k).wait_send()
        hole_copy(k).start()
    for k in arrived[:-LAST]:
        amp_copy(k).wait_recv()
    for i, k in enumerate(sent[len(staying):]):
        amp_copy(k).wait_send()
        hole_copy(k).start()
        if STEP <= i + 1 < STEP + LAST:
            amp_copy(arrived[i + 1 - STEP - LAST]).wait_recv()
    keep_hole = pltpu.make_async_copy(own_hole.at[own_pairs], hole_all.at[:, mine], local_sem.at[1])
    keep_hole.start()

    load_chol.wait()
    keep_amp.wait()

    def one_pair(p, carry):
        result[p] = jnp.zeros((full, full), jnp.float32)

        def one_vector(q, c):
            vector = chol_v[q]
            mixed = jnp.dot(vector, amp_all[p], preferred_element_type=jnp.float32).astype(jnp.bfloat16)
            result[p] += lax.dot_general(
                mixed, vector, (((1,), (1,)), ((), ())), preferred_element_type=jnp.float32
            )
            return c

        lax.fori_loop(0, n_vec, one_vector, 0)
        return carry

    lax.fori_loop(0, pairs, one_pair, 0)

    def finish(k):
        at = rows_of(me ^ k)

        def one(p, carry):
            result[p, at, :] = (hole_all[p, at, :].astype(jnp.float32) + result[p, at, :]) * inverse[p, at, :]
            return carry

        lax.fori_loop(0, pairs, one, 0)

    keep_hole.wait()
    finish(0)
    for even, odd in zip(*hole_order):
        k = by_core(core, even, odd)
        hole_copy(k).wait_recv()
        finish(k)
    for k in range(1, n):
        hole_copy(k).wait_send()


def write_kernel(result, out, sems):
    pieces = sems.shape[0]
    size = result.shape[0] // pieces
    puts = [
        pltpu.make_async_copy(result.at[pl.ds(i * size, size)], out.at[pl.ds(i * size, size)], sems.at[i])
        for i in range(pieces)
    ]
    for put in puts:
        put.start()
    for put in puts:
        put.wait()


def exchange_and_contract(amplitudes, ladder, cholesky, pair_ids, occ_energy, vir_energy):
    n = lax.axis_size("pair")
    total, rows, width = amplitudes.shape
    pairs = total // n
    full = rows * n
    anywhere = pl.BlockSpec(memory_space=pl.ANY)
    in_hbm = pl.BlockSpec(memory_space=pltpu.HBM)
    in_vmem = pl.BlockSpec(memory_space=pltpu.VMEM)
    result, _ = pl.pallas_call(
        functools.partial(residual_kernel, n),
        out_shape=[
            pltpu.VMEM((pairs, full, full), jnp.float32),
            jax.ShapeDtypeStruct(amplitudes.shape, jnp.bfloat16),
        ],
        in_specs=[in_hbm] * 6,
        out_specs=[in_vmem, in_hbm],
        scratch_shapes=[
            pltpu.VMEM(amplitudes.shape, jnp.bfloat16),
            pltpu.VMEM((total * rows, 128), jnp.float32),
            pltpu.VMEM(ladder.shape, jnp.bfloat16),
            pltpu.VMEM(cholesky.shape, jnp.bfloat16),
            pltpu.VMEM((pairs, full, width), jnp.bfloat16),
            pltpu.VMEM((pairs, full, width), jnp.bfloat16),
            pltpu.VMEM((pairs, full, full), jnp.float32),
            pltpu.VMEM((1, full), jnp.float32),
            pltpu.SMEM(pair_ids.shape, jnp.int32),
            pltpu.SMEM(occ_energy.shape, jnp.float32),
            pltpu.SemaphoreType.DMA((n,)),
            pltpu.SemaphoreType.DMA((n,)),
            pltpu.SemaphoreType.DMA((n,)),
            pltpu.SemaphoreType.DMA((n,)),
            pltpu.SemaphoreType.DMA((7,)),
            pltpu.SemaphoreType.REGULAR((n.bit_length(),)),
        ],
        compiler_params=pltpu.CompilerParams(
            collective_id=0, has_side_effects=True, vmem_limit_bytes=VMEM_BYTES - 4 * pairs * full * full
        ),
    )(amplitudes, ladder, cholesky, pair_ids, occ_energy, vir_energy.reshape(1, -1))
    return pl.pallas_call(
        write_kernel,
        out_shape=jax.ShapeDtypeStruct((pairs, full, full), jnp.float32),
        in_specs=[in_vmem],
        out_specs=in_hbm,
        scratch_shapes=[pltpu.SemaphoreType.DMA((pairs,))],
        compiler_params=pltpu.CompilerParams(vmem_limit_bytes=8 * 1024 * 1024),
    )(result)


def exchange_plain(amplitudes, ladder, cholesky):
    flat = amplitudes.reshape(amplitudes.shape[0], -1)
    hole = jnp.dot(ladder, flat, preferred_element_type=jnp.float32).astype(jnp.bfloat16)
    hole = hole.reshape(amplitudes.shape)
    pair_amps = lax.all_to_all(amplitudes, "pair", split_axis=0, concat_axis=1, tiled=True)
    pair_hole = lax.all_to_all(hole, "pair", split_axis=0, concat_axis=1, tiled=True)
    mixed = jnp.einsum(
        "qac,pcd->qpad", cholesky, pair_amps, preferred_element_type=jnp.float32
    ).astype(jnp.bfloat16)
    particle = jnp.einsum("qpad,qbd->pab", mixed, cholesky, preferred_element_type=jnp.float32)
    return pair_hole, particle


def shards(amplitudes, ladder, cholesky, pair_ids, occ_energy, vir_energy):
    n = lax.axis_size("pair")
    n_aux = lax.axis_size("aux")
    half_width = amplitudes.shape[2] // n_aux
    aux_index = lax.axis_index("aux")
    aligned = amplitudes.shape[1] % 16 == 0 and n & (n - 1) == 0 and n >= 4
    if aligned and n_aux == 1:
        return exchange_and_contract(amplitudes, ladder, cholesky, pair_ids, occ_energy, vir_energy)
    hole, particle = exchange_plain(amplitudes, ladder, cholesky)
    if n_aux > 1:
        hole = lax.dynamic_slice_in_dim(hole, aux_index * half_width, half_width, 2)
        particle = lax.psum_scatter(particle, "aux", scatter_dimension=2, tiled=True)
    orbitals = jnp.arange(NO, dtype=jnp.int32)
    first_hot = (pair_ids // NO)[:, None] == orbitals[None, :]
    second_hot = (pair_ids % NO)[:, None] == orbitals[None, :]
    hot = first_hot.astype(jnp.float32) + second_hot.astype(jnp.float32)
    occ_sum = jnp.sum(hot * occ_energy[None, :], axis=1)
    vir_cols = lax.dynamic_slice_in_dim(vir_energy, aux_index * half_width, half_width, 0)
    denominator = vir_energy[None, :, None] + vir_cols[None, None, :] - occ_sum[:, None, None]
    return (hole.astype(jnp.float32) + particle) / denominator


def solution(mesh):
    in_specs = (P(None, "pair", None), P(), P("aux", None, None), P("pair"), P(), P())
    out_specs = P("pair", None, "aux")
    return jax.shard_map(shards, mesh=mesh, in_specs=in_specs, out_specs=out_specs, check_vma=False)
```

```python
import functools

import jax
import jax.numpy as jnp
from jax import lax
from jax.experimental import pallas as pl
from jax.experimental.pallas import tpu as pltpu
from jax.sharding import PartitionSpec as P

NO = 16
VMEM_BYTES = 67043328
LAST = 4
STEP = 4
MESH = pl.DeviceIdType.MESH


def by_core(core, even, odd):
    return even + core * (odd - even)


def weave(first, second):
    return [k for pair in zip(first, second) for k in pair]


def amp_orders(n, mid):
    half, quarter = n // 2, n // 4
    chip = list(range(1, quarter))
    beside = [quarter + a for a in range(quarter)]
    near = [half + quarter * mid + a for a in range(quarter)]
    far = [half + quarter * (1 - mid) + a for a in range(quarter)]
    lead = quarter // 4
    outward = near[:lead] + weave(far, near[lead:]) + far[quarter - lead:]
    outer_order = weave(outward[:quarter], beside) + outward[quarter:] + chip
    middle_rest = beside + [half + a for a in range(quarter)] + chip
    return outer_order, middle_rest


def hole_orders(n, mid):
    half, quarter = n // 2, n // 4
    near = [half + quarter * mid + a for a in reversed(range(quarter))]
    far = [half + quarter * (1 - mid) + a for a in reversed(range(quarter))]
    lead = quarter // 4
    inward = far[:lead] + weave(near, far[lead:]) + near[quarter - lead:]
    staying = [a + b for a in range(quarter) for b in (quarter, 0) if a + b]
    return staying + inward, inward + staying


def arrival_orders(n):
    half, quarter = n // 2, n // 4
    crossing = [a + b for a in range(quarter) for b in (half + quarter, half)]
    staying = [a + b for a in range(quarter) for b in (quarter, 0) if a + b]
    cross = [k for k in crossing if k % 2 == 0], [k for k in crossing if k % 2]
    stay = [k for k in staying if k % 2 == 0], [k for k in staying if k % 2]
    amps = cross[0] + stay[1] + stay[0] + cross[1], stay[0] + cross[1] + stay[1] + cross[0]
    cross = cross[0][::-1], cross[1][::-1]
    holes = stay[0] + cross[1] + stay[1] + cross[0], stay[1] + cross[0] + stay[0] + cross[1]
    return amps, holes


def residual_kernel(
    n, amps, ladder, chol, pair_ids, occ, vir, result, own_hole,
    amp_own, wide, ladder_v, chol_v, amp_all, hole_all, inverse, vir_v, ids_s, occ_s,
    amp_send, amp_recv, hole_send, hole_recv, local_sem, entry_sem,
):
    total, rows, width = amps.shape
    pairs = total // n
    full = rows * n
    n_vec = chol.shape[0]
    me = lax.axis_index("pair")
    core = me % 2
    half, quarter = n // 2, n // 4
    mid = (me // quarter + 1) // 2 % 2
    outer_order, middle_rest = amp_orders(n, mid)
    mine = pl.ds(pl.multiple_of(me * rows, rows), rows)
    own_pairs = pl.ds(me * pairs, pairs)

    def rows_of(source):
        return pl.ds(pl.multiple_of(source * rows, rows), rows)

    def amp_copy(k):
        dest = me ^ k
        return pltpu.make_async_remote_copy(
            amps.at[pl.ds(dest * pairs, pairs)], amp_all.at[:, mine],
            amp_send.at[k], amp_recv.at[k], device_id={"pair": dest}, device_id_type=MESH,
        )

    def hole_copy(k):
        dest = me ^ k
        return pltpu.make_async_remote_copy(
            own_hole.at[pl.ds(dest * pairs, pairs)], hole_all.at[:, mine],
            hole_send.at[k], hole_recv.at[k], device_id={"pair": dest}, device_id_type=MESH,
        )

    load_amp = pltpu.make_async_copy(amps, amp_own, local_sem.at[0])
    load_ladder = pltpu.make_async_copy(ladder, ladder_v, local_sem.at[1])
    load_chol = pltpu.make_async_copy(chol, chol_v, local_sem.at[2])
    keep_amp = pltpu.make_async_copy(amps.at[own_pairs], amp_all.at[:, mine], local_sem.at[3])
    load_ids = pltpu.make_async_copy(pair_ids, ids_s, local_sem.at[4])
    load_occ = pltpu.make_async_copy(occ, occ_s, local_sem.at[5])
    load_vir = pltpu.make_async_copy(vir, vir_v, local_sem.at[6])

    def tell(sem, k):
        pl.semaphore_signal(sem, inc=1, device_id={"pair": me ^ k}, device_id_type=MESH)

    barrier = pltpu.get_barrier_semaphore()
    low_bits = [1 << i for i in range(quarter.bit_length() - 1)]
    across, along, last = range(len(low_bits), len(low_bits) + 3)

    @pl.when(mid == 1)
    def _():
        tell(barrier, half + quarter)

    for k in low_bits:
        tell(barrier, k)

    @pl.when(mid == 1)
    def _():
        tell(barrier, quarter)

    load_amp.start()
    load_ladder.start()
    load_chol.start()
    keep_amp.start()
    load_ids.start()
    load_occ.start()
    load_vir.start()

    pl.semaphore_wait(barrier, len(low_bits) + 1)

    def start_near(first, last):
        @pl.when(mid == 1)
        def _():
            for a in range(first, last):
                amp_copy(half + quarter + a).start()

    start_near(0, 1)
    for i, k in enumerate(low_bits):
        tell(entry_sem.at[i], k)
        pl.semaphore_wait(entry_sem.at[i], 1)
        start_near(k, 2 * k)

    @pl.when(mid == 1)
    def _():
        tell(entry_sem.at[across], half + quarter)
        pl.semaphore_wait(entry_sem.at[across], 2)
        tell(entry_sem.at[along], half + quarter)
        tell(entry_sem.at[along], quarter)
        pl.semaphore_wait(entry_sem.at[along], 1)
        tell(entry_sem.at[last], quarter)

    @pl.when(mid == 0)
    def _():
        tell(entry_sem.at[across], quarter)
        pl.semaphore_wait(entry_sem.at[along], 1)
        pl.semaphore_wait(entry_sem.at[last], 1)

    @pl.when(mid == 1)
    def _():
        for k in middle_rest:
            amp_copy(k).start()

    @pl.when(mid == 0)
    def _():
        for k in outer_order:
            amp_copy(k).start()

    load_amp.wait()
    load_ladder.wait()
    block = 16
    lanes = 128

    def columns(j, carry):
        cols = pl.ds(pl.multiple_of(j * lanes, lanes), lanes)

        def widen(i, c):
            part = amp_own[pl.ds(i * block, block), :, cols].astype(jnp.float32)
            wide[pl.ds(pl.multiple_of(i * block * rows, block * rows), block * rows), :] = part.reshape(block * rows, lanes)
            return c

        lax.fori_loop(0, total // block, widen, 0)

        def one_row(a, c):
            sel = pl.ds(a, total, stride=rows)
            value = wide[sel, :].astype(jnp.bfloat16)
            wide[sel, :] = jnp.dot(ladder_v[...], value, preferred_element_type=jnp.float32)
            return c

        lax.fori_loop(0, rows, one_row, 0)

        def narrow(i, c):
            part = wide[pl.ds(pl.multiple_of(i * block * rows, block * rows), block * rows), :].astype(jnp.bfloat16)
            amp_own[pl.ds(i * block, block), :, cols] = part.reshape(block, rows, lanes)
            return c

        lax.fori_loop(0, total // block, narrow, 0)
        return carry

    lax.fori_loop(0, width // lanes, columns, 0)
    store_hole = pltpu.make_async_copy(amp_own, own_hole, local_sem.at[0])
    store_hole.start()
    store_hole.wait()

    load_ids.wait()
    load_occ.wait()
    load_vir.wait()

    def one_inverse(p, carry):
        pair = ids_s[p]
        shift = occ_s[pair // NO] + occ_s[pair % NO]

        def add_virtuals(i, c):
            at = pl.ds(pl.multiple_of(i * lanes, lanes), lanes)
            row = vir_v[:, at]
            diagonal = lax.broadcasted_iota(jnp.int32, (lanes, lanes), 0) == lax.broadcasted_iota(jnp.int32, (lanes, lanes), 1)
            column = jnp.sum(jnp.where(diagonal, row, 0.0), axis=1, keepdims=True)
            inverse[p, at, :] = 1.0 / (column + vir_v[...] - shift)
            return c

        lax.fori_loop(0, full // lanes, add_virtuals, 0)
        return carry

    lax.fori_loop(0, pairs, one_inverse, 0)

    amp_order, hole_order = arrival_orders(n)
    arrived = [by_core(core, even, odd) for even, odd in zip(*amp_order)]
    sent = [by_core(core, even, odd) for even, odd in zip(*hole_orders(n, mid))]
    staying = half - 1
    for k in sent[:staying]:
        amp_copy(k).wait_send()
        hole_copy(k).start()
    for k in arrived[:-LAST]:
        amp_copy(k).wait_recv()
    for i, k in enumerate(sent[staying:]):
        amp_copy(k).wait_send()
        hole_copy(k).start()
        if STEP <= i + 1 < STEP + LAST:
            amp_copy(arrived[i + 1 - STEP - LAST]).wait_recv()
    keep_hole = pltpu.make_async_copy(own_hole.at[own_pairs], hole_all.at[:, mine], local_sem.at[1])
    keep_hole.start()

    load_chol.wait()
    keep_amp.wait()

    def one_pair(p, carry):
        result[p] = jnp.zeros((full, full), jnp.float32)

        def one_vector(q, c):
            vector = chol_v[q]
            mixed = jnp.dot(vector, amp_all[p], preferred_element_type=jnp.float32).astype(jnp.bfloat16)
            result[p] += lax.dot_general(
                mixed, vector, (((1,), (1,)), ((), ())), preferred_element_type=jnp.float32
            )
            return c

        lax.fori_loop(0, n_vec, one_vector, 0)
        return carry

    lax.fori_loop(0, pairs, one_pair, 0)

    def finish(k):
        at = rows_of(me ^ k)

        def one(p, carry):
            result[p, at, :] = (hole_all[p, at, :].astype(jnp.float32) + result[p, at, :]) * inverse[p, at, :]
            return carry

        lax.fori_loop(0, pairs, one, 0)

    keep_hole.wait()
    finish(0)
    for even, odd in zip(*hole_order):
        k = by_core(core, even, odd)
        hole_copy(k).wait_recv()
        finish(k)
    for k in range(1, n):
        hole_copy(k).wait_send()


def write_kernel(result, out, sems):
    pieces = sems.shape[0]
    size = result.shape[0] // pieces
    puts = [
        pltpu.make_async_copy(result.at[pl.ds(i * size, size)], out.at[pl.ds(i * size, size)], sems.at[i])
        for i in range(pieces)
    ]
    for put in puts:
        put.start()
    for put in puts:
        put.wait()


def exchange_and_contract(amplitudes, ladder, cholesky, pair_ids, occ_energy, vir_energy):
    n = lax.axis_size("pair")
    total, rows, width = amplitudes.shape
    pairs = total // n
    full = rows * n
    anywhere = pl.BlockSpec(memory_space=pl.ANY)
    in_hbm = pl.BlockSpec(memory_space=pltpu.HBM)
    in_vmem = pl.BlockSpec(memory_space=pltpu.VMEM)
    result, _ = pl.pallas_call(
        functools.partial(residual_kernel, n),
        out_shape=[
            pltpu.VMEM((pairs, full, full), jnp.float32),
            jax.ShapeDtypeStruct(amplitudes.shape, jnp.bfloat16),
        ],
        in_specs=[in_hbm] * 6,
        out_specs=[in_vmem, in_hbm],
        scratch_shapes=[
            pltpu.VMEM(amplitudes.shape, jnp.bfloat16),
            pltpu.VMEM((total * rows, 128), jnp.float32),
            pltpu.VMEM(ladder.shape, jnp.bfloat16),
            pltpu.VMEM(cholesky.shape, jnp.bfloat16),
            pltpu.VMEM((pairs, full, width), jnp.bfloat16),
            pltpu.VMEM((pairs, full, width), jnp.bfloat16),
            pltpu.VMEM((pairs, full, full), jnp.float32),
            pltpu.VMEM((1, full), jnp.float32),
            pltpu.SMEM(pair_ids.shape, jnp.int32),
            pltpu.SMEM(occ_energy.shape, jnp.float32),
            pltpu.SemaphoreType.DMA((n,)),
            pltpu.SemaphoreType.DMA((n,)),
            pltpu.SemaphoreType.DMA((n,)),
            pltpu.SemaphoreType.DMA((n,)),
            pltpu.SemaphoreType.DMA((7,)),
            pltpu.SemaphoreType.REGULAR((n.bit_length(),)),
        ],
        compiler_params=pltpu.CompilerParams(
            collective_id=0, has_side_effects=True, vmem_limit_bytes=VMEM_BYTES - 4 * pairs * full * full
        ),
    )(amplitudes, ladder, cholesky, pair_ids, occ_energy, vir_energy.reshape(1, -1))
    return pl.pallas_call(
        write_kernel,
        out_shape=jax.ShapeDtypeStruct((pairs, full, full), jnp.float32),
        in_specs=[in_vmem],
        out_specs=in_hbm,
        scratch_shapes=[pltpu.SemaphoreType.DMA((pairs,))],
        compiler_params=pltpu.CompilerParams(vmem_limit_bytes=8 * 1024 * 1024),
    )(result)


def exchange_plain(amplitudes, ladder, cholesky):
    flat = amplitudes.reshape(amplitudes.shape[0], -1)
    hole = jnp.dot(ladder, flat, preferred_element_type=jnp.float32).astype(jnp.bfloat16)
    hole = hole.reshape(amplitudes.shape)
    pair_amps = lax.all_to_all(amplitudes, "pair", split_axis=0, concat_axis=1, tiled=True)
    pair_hole = lax.all_to_all(hole, "pair", split_axis=0, concat_axis=1, tiled=True)
    mixed = jnp.einsum(
        "qac,pcd->qpad", cholesky, pair_amps, preferred_element_type=jnp.float32
    ).astype(jnp.bfloat16)
    particle = jnp.einsum("qpad,qbd->pab", mixed, cholesky, preferred_element_type=jnp.float32)
    return pair_hole, particle


def shards(amplitudes, ladder, cholesky, pair_ids, occ_energy, vir_energy):
    n = lax.axis_size("pair")
    n_aux = lax.axis_size("aux")
    half_width = amplitudes.shape[2] // n_aux
    aux_index = lax.axis_index("aux")
    aligned = amplitudes.shape[1] % 16 == 0 and n & (n - 1) == 0 and n >= 4
    if aligned and n_aux == 1:
        return exchange_and_contract(amplitudes, ladder, cholesky, pair_ids, occ_energy, vir_energy)
    hole, particle = exchange_plain(amplitudes, ladder, cholesky)
    if n_aux > 1:
        hole = lax.dynamic_slice_in_dim(hole, aux_index * half_width, half_width, 2)
        particle = lax.psum_scatter(particle, "aux", scatter_dimension=2, tiled=True)
    orbitals = jnp.arange(NO, dtype=jnp.int32)
    first_hot = (pair_ids // NO)[:, None] == orbitals[None, :]
    second_hot = (pair_ids % NO)[:, None] == orbitals[None, :]
    hot = first_hot.astype(jnp.float32) + second_hot.astype(jnp.float32)
    occ_sum = jnp.sum(hot * occ_energy[None, :], axis=1)
    vir_cols = lax.dynamic_slice_in_dim(vir_energy, aux_index * half_width, half_width, 0)
    denominator = vir_energy[None, :, None] + vir_cols[None, None, :] - occ_sum[:, None, None]
    return (hole.astype(jnp.float32) + particle) / denominator


def solution(mesh):
    in_specs = (P(None, "pair", None), P(), P("aux", None, None), P("pair"), P(), P())
    out_specs = P("pair", None, "aux")
    return jax.shard_map(shards, mesh=mesh, in_specs=in_specs, out_specs=out_specs, check_vma=False)
```

```python
import functools

import jax
import jax.numpy as jnp
from jax import lax
from jax.experimental import pallas as pl
from jax.experimental.pallas import tpu as pltpu
from jax.sharding import PartitionSpec as P

NO = 16
VMEM_BYTES = 67043328
STEP = 8
MESH = pl.DeviceIdType.MESH


def by_core(core, even, odd):
    return even + core * (odd - even)


def weave(first, second):
    return [k for pair in zip(first, second) for k in pair]


def amp_orders(n, mid):
    half, quarter = n // 2, n // 4
    chip = list(range(1, quarter))
    beside = [quarter + a for a in range(quarter)]
    near = [half + quarter * mid + a for a in range(quarter)]
    far = [half + quarter * (1 - mid) + a for a in range(quarter)]
    lead = quarter // 4
    outward = near[:lead] + weave(far, near[lead:]) + far[quarter - lead:]
    outer_order = weave(outward[:quarter], beside) + outward[quarter:] + chip
    middle_rest = beside + [half + a for a in range(quarter)] + chip
    return outer_order, middle_rest


def hole_orders(n, mid):
    half, quarter = n // 2, n // 4
    near = [half + quarter * mid + a for a in reversed(range(quarter))]
    far = [half + quarter * (1 - mid) + a for a in reversed(range(quarter))]
    lead = quarter // 4
    inward = far[:lead] + weave(near, far[lead:]) + near[quarter - lead:]
    staying = [a + b for a in range(quarter) for b in (quarter, 0) if a + b]
    return staying + inward, inward + staying


def residual_kernel(
    n, amps, ladder, chol, pair_ids, occ, vir, result, own_hole,
    amp_own, wide, ladder_v, chol_v, amp_all, hole_all, inverse, vir_v, ids_s, occ_s,
    send_sem, amp_recv, hole_recv, local_sem, entry_sem,
):
    total, rows, width = amps.shape
    pairs = total // n
    full = rows * n
    n_vec = chol.shape[0]
    me = lax.axis_index("pair")
    core = me % 2
    half, quarter = n // 2, n // 4
    mid = (me // quarter + 1) // 2 % 2
    outer_order, middle_rest = amp_orders(n, mid)
    mine = pl.ds(pl.multiple_of(me * rows, rows), rows)
    own_pairs = pl.ds(me * pairs, pairs)

    def rows_of(source):
        return pl.ds(pl.multiple_of(source * rows, rows), rows)

    def amp_copy(k):
        dest = me ^ k
        last = k // half * (k % quarter // (quarter // 2)) * core
        return pltpu.make_async_remote_copy(
            amps.at[pl.ds(dest * pairs, pairs)], amp_all.at[:, mine],
            send_sem.at[0], amp_recv.at[last], device_id={"pair": dest}, device_id_type=MESH,
        )

    def hole_copy(k):
        dest = me ^ k
        cross = k // half
        single = (1 - core) * cross
        slot = single * (k % quarter // 2 * 2 + k // quarter % 2) + (1 - single) * (quarter + 2 * core + cross)
        return pltpu.make_async_remote_copy(
            own_hole.at[pl.ds(dest * pairs, pairs)], hole_all.at[:, mine],
            send_sem.at[1], hole_recv.at[slot], device_id={"pair": dest}, device_id_type=MESH,
        )

    def wait_blocks(ref, count, sem):
        part = ref.at[:, pl.ds(0, count * rows)]
        pltpu.make_async_copy(part, part, sem).wait()

    def wait_sent(ref, sem):
        part = ref.at[pl.ds(0, (n - 1) * pairs)]
        pltpu.make_async_copy(part, part, sem).wait()

    load_amp = pltpu.make_async_copy(amps, amp_own, local_sem.at[0])
    load_ladder = pltpu.make_async_copy(ladder, ladder_v, local_sem.at[1])
    load_chol = pltpu.make_async_copy(chol, chol_v, local_sem.at[2])
    keep_amp = pltpu.make_async_copy(amps.at[own_pairs], amp_all.at[:, mine], local_sem.at[3])
    load_ids = pltpu.make_async_copy(pair_ids, ids_s, local_sem.at[4])
    load_occ = pltpu.make_async_copy(occ, occ_s, local_sem.at[5])
    load_vir = pltpu.make_async_copy(vir, vir_v, local_sem.at[6])

    def tell(sem, k):
        pl.semaphore_signal(sem, inc=1, device_id={"pair": me ^ k}, device_id_type=MESH)

    barrier = pltpu.get_barrier_semaphore()
    low_bits = [1 << i for i in range(quarter.bit_length() - 1)]
    across, along, last = range(len(low_bits), len(low_bits) + 3)

    @pl.when(mid == 1)
    def _():
        tell(barrier, half + quarter)

    for k in low_bits:
        tell(barrier, k)

    @pl.when(mid == 1)
    def _():
        tell(barrier, quarter)

    load_amp.start()
    load_ladder.start()
    load_chol.start()
    keep_amp.start()
    load_ids.start()
    load_occ.start()
    load_vir.start()

    pl.semaphore_wait(barrier, len(low_bits) + 1)

    def start_near(first, last):
        @pl.when(mid == 1)
        def _():
            for a in range(first, last):
                amp_copy(half + quarter + a).start()

    start_near(0, 1)
    for i, k in enumerate(low_bits):
        tell(entry_sem.at[i], k)
        pl.semaphore_wait(entry_sem.at[i], 1)
        start_near(k, 2 * k)

    @pl.when(mid == 1)
    def _():
        tell(entry_sem.at[across], half + quarter)
        pl.semaphore_wait(entry_sem.at[across], 2)
        tell(entry_sem.at[along], half + quarter)
        tell(entry_sem.at[along], quarter)
        pl.semaphore_wait(entry_sem.at[along], 1)
        tell(entry_sem.at[last], quarter)

    @pl.when(mid == 0)
    def _():
        tell(entry_sem.at[across], quarter)
        pl.semaphore_wait(entry_sem.at[along], 1)
        pl.semaphore_wait(entry_sem.at[last], 1)

    @pl.when(mid == 1)
    def _():
        for k in middle_rest:
            amp_copy(k).start()

    @pl.when(mid == 0)
    def _():
        for k in outer_order:
            amp_copy(k).start()

    load_amp.wait()
    load_ladder.wait()
    block = 16
    lanes = 128

    def columns(j, carry):
        cols = pl.ds(pl.multiple_of(j * lanes, lanes), lanes)

        def widen(i, c):
            part = amp_own[pl.ds(i * block, block), :, cols].astype(jnp.float32)
            wide[pl.ds(pl.multiple_of(i * block * rows, block * rows), block * rows), :] = part.reshape(block * rows, lanes)
            return c

        lax.fori_loop(0, total // block, widen, 0)

        def one_row(a, c):
            sel = pl.ds(a, total, stride=rows)
            value = wide[sel, :].astype(jnp.bfloat16)
            wide[sel, :] = jnp.dot(ladder_v[...], value, preferred_element_type=jnp.float32)
            return c

        lax.fori_loop(0, rows, one_row, 0)

        def narrow(i, c):
            part = wide[pl.ds(pl.multiple_of(i * block * rows, block * rows), block * rows), :].astype(jnp.bfloat16)
            amp_own[pl.ds(i * block, block), :, cols] = part.reshape(block, rows, lanes)
            return c

        lax.fori_loop(0, total // block, narrow, 0)
        return carry

    lax.fori_loop(0, width // lanes, columns, 0)
    store_hole = pltpu.make_async_copy(amp_own, own_hole, local_sem.at[0])
    store_hole.start()
    store_hole.wait()

    load_ids.wait()
    load_occ.wait()
    load_vir.wait()

    def one_inverse(p, carry):
        pair = ids_s[p]
        shift = occ_s[pair // NO] + occ_s[pair % NO]

        def add_virtuals(i, c):
            at = pl.ds(pl.multiple_of(i * lanes, lanes), lanes)
            row = vir_v[:, at]
            diagonal = lax.broadcasted_iota(jnp.int32, (lanes, lanes), 0) == lax.broadcasted_iota(jnp.int32, (lanes, lanes), 1)
            column = jnp.sum(jnp.where(diagonal, row, 0.0), axis=1, keepdims=True)
            inverse[p, at, :] = 1.0 / (column + vir_v[...] - shift)
            return c

        lax.fori_loop(0, full // lanes, add_virtuals, 0)
        return carry

    lax.fori_loop(0, pairs, one_inverse, 0)

    wait_sent(amps, send_sem.at[0])
    sent = [by_core(core, even, odd) for even, odd in zip(*hole_orders(n, mid))]
    for k in sent[:half - 1]:
        hole_copy(k).start()
    wait_blocks(amp_all, n - 1 - half // 4, amp_recv.at[0])
    for k in sent[half - 1:half - 1 + STEP]:
        hole_copy(k).start()
    wait_blocks(amp_all, half // 4, amp_recv.at[1])
    for k in sent[half - 1 + STEP:]:
        hole_copy(k).start()
    keep_hole = pltpu.make_async_copy(own_hole.at[own_pairs], hole_all.at[:, mine], local_sem.at[1])
    keep_hole.start()

    load_chol.wait()
    keep_amp.wait()

    def one_pair(p, carry):
        result[p] = jnp.zeros((full, full), jnp.float32)

        def one_vector(q, c):
            vector = chol_v[q]
            mixed = jnp.dot(vector, amp_all[p], preferred_element_type=jnp.float32).astype(jnp.bfloat16)
            result[p] += lax.dot_general(
                mixed, vector, (((1,), (1,)), ((), ())), preferred_element_type=jnp.float32
            )
            return c

        lax.fori_loop(0, n_vec, one_vector, 0)
        return carry

    lax.fori_loop(0, pairs, one_pair, 0)

    def finish(k):
        at = rows_of(me ^ k)

        def one(p, carry):
            result[p, at, :] = (hole_all[p, at, :].astype(jnp.float32) + result[p, at, :]) * inverse[p, at, :]
            return carry

        lax.fori_loop(0, pairs, one, 0)

    keep_hole.wait()

    def finish_some(base):
        def one(i, carry):
            finish(base + 2 * i)
            return carry

        lax.fori_loop(0, half // 2, one, 0)

    def wait_staying(slot, fewer):
        @pl.when(fewer == 1)
        def _():
            wait_blocks(hole_all, half // 2 - 1, hole_recv.at[slot])

        @pl.when(fewer == 0)
        def _():
            wait_blocks(hole_all, half // 2, hole_recv.at[slot])

    wait_staying(quarter, 1 - core)
    finish_some(core)
    wait_blocks(hole_all, half // 2, hole_recv.at[quarter + 3])
    finish_some(half + 1 - core)
    wait_staying(quarter + 2, core)
    finish_some(1 - core)
    for a in reversed(range(quarter // 2)):
        for step in range(2):
            wait_blocks(hole_all, 1, hole_recv.at[2 * a + step])
            finish(half + quarter * step + 2 * a + core)
    wait_sent(own_hole, send_sem.at[1])


def write_kernel(result, out, sems):
    pieces = sems.shape[0]
    size = result.shape[0] // pieces
    puts = [
        pltpu.make_async_copy(result.at[pl.ds(i * size, size)], out.at[pl.ds(i * size, size)], sems.at[i])
        for i in range(pieces)
    ]
    for put in puts:
        put.start()
    for put in puts:
        put.wait()


def exchange_and_contract(amplitudes, ladder, cholesky, pair_ids, occ_energy, vir_energy):
    n = lax.axis_size("pair")
    total, rows, width = amplitudes.shape
    pairs = total // n
    full = rows * n
    anywhere = pl.BlockSpec(memory_space=pl.ANY)
    in_hbm = pl.BlockSpec(memory_space=pltpu.HBM)
    in_vmem = pl.BlockSpec(memory_space=pltpu.VMEM)
    result, _ = pl.pallas_call(
        functools.partial(residual_kernel, n),
        out_shape=[
            pltpu.VMEM((pairs, full, full), jnp.float32),
            jax.ShapeDtypeStruct(amplitudes.shape, jnp.bfloat16),
        ],
        in_specs=[in_hbm] * 6,
        out_specs=[in_vmem, in_hbm],
        scratch_shapes=[
            pltpu.VMEM(amplitudes.shape, jnp.bfloat16),
            pltpu.VMEM((total * rows, 128), jnp.float32),
            pltpu.VMEM(ladder.shape, jnp.bfloat16),
            pltpu.VMEM(cholesky.shape, jnp.bfloat16),
            pltpu.VMEM((pairs, full, width), jnp.bfloat16),
            pltpu.VMEM((pairs, full, width), jnp.bfloat16),
            pltpu.VMEM((pairs, full, full), jnp.float32),
            pltpu.VMEM((1, full), jnp.float32),
            pltpu.SMEM(pair_ids.shape, jnp.int32),
            pltpu.SMEM(occ_energy.shape, jnp.float32),
            pltpu.SemaphoreType.DMA((2,)),
            pltpu.SemaphoreType.DMA((2,)),
            pltpu.SemaphoreType.DMA((n // 4 + 4,)),
            pltpu.SemaphoreType.DMA((7,)),
            pltpu.SemaphoreType.REGULAR((n.bit_length(),)),
        ],
        compiler_params=pltpu.CompilerParams(
            collective_id=0, has_side_effects=True, vmem_limit_bytes=VMEM_BYTES - 4 * pairs * full * full
        ),
    )(amplitudes, ladder, cholesky, pair_ids, occ_energy, vir_energy.reshape(1, -1))
    return pl.pallas_call(
        write_kernel,
        out_shape=jax.ShapeDtypeStruct((pairs, full, full), jnp.float32),
        in_specs=[in_vmem],
        out_specs=in_hbm,
        scratch_shapes=[pltpu.SemaphoreType.DMA((pairs,))],
        compiler_params=pltpu.CompilerParams(vmem_limit_bytes=8 * 1024 * 1024),
    )(result)


def exchange_plain(amplitudes, ladder, cholesky):
    flat = amplitudes.reshape(amplitudes.shape[0], -1)
    hole = jnp.dot(ladder, flat, preferred_element_type=jnp.float32).astype(jnp.bfloat16)
    hole = hole.reshape(amplitudes.shape)
    pair_amps = lax.all_to_all(amplitudes, "pair", split_axis=0, concat_axis=1, tiled=True)
    pair_hole = lax.all_to_all(hole, "pair", split_axis=0, concat_axis=1, tiled=True)
    mixed = jnp.einsum(
        "qac,pcd->qpad", cholesky, pair_amps, preferred_element_type=jnp.float32
    ).astype(jnp.bfloat16)
    particle = jnp.einsum("qpad,qbd->pab", mixed, cholesky, preferred_element_type=jnp.float32)
    return pair_hole, particle


def shards(amplitudes, ladder, cholesky, pair_ids, occ_energy, vir_energy):
    n = lax.axis_size("pair")
    n_aux = lax.axis_size("aux")
    half_width = amplitudes.shape[2] // n_aux
    aux_index = lax.axis_index("aux")
    aligned = amplitudes.shape[1] % 16 == 0 and n & (n - 1) == 0 and n >= 16
    if aligned and n_aux == 1:
        return exchange_and_contract(amplitudes, ladder, cholesky, pair_ids, occ_energy, vir_energy)
    hole, particle = exchange_plain(amplitudes, ladder, cholesky)
    if n_aux > 1:
        hole = lax.dynamic_slice_in_dim(hole, aux_index * half_width, half_width, 2)
        particle = lax.psum_scatter(particle, "aux", scatter_dimension=2, tiled=True)
    orbitals = jnp.arange(NO, dtype=jnp.int32)
    first_hot = (pair_ids // NO)[:, None] == orbitals[None, :]
    second_hot = (pair_ids % NO)[:, None] == orbitals[None, :]
    hot = first_hot.astype(jnp.float32) + second_hot.astype(jnp.float32)
    occ_sum = jnp.sum(hot * occ_energy[None, :], axis=1)
    vir_cols = lax.dynamic_slice_in_dim(vir_energy, aux_index * half_width, half_width, 0)
    denominator = vir_energy[None, :, None] + vir_cols[None, None, :] - occ_sum[:, None, None]
    return (hole.astype(jnp.float32) + particle) / denominator


def solution(mesh):
    in_specs = (P(None, "pair", None), P(), P("aux", None, None), P("pair"), P(), P())
    out_specs = P("pair", None, "aux")
    return jax.shard_map(shards, mesh=mesh, in_specs=in_specs, out_specs=out_specs, check_vma=False)
```

```python
import functools

import jax
import jax.numpy as jnp
from jax import lax
from jax.experimental import pallas as pl
from jax.experimental.pallas import tpu as pltpu
from jax.sharding import PartitionSpec as P

NO = 16
VMEM_BYTES = 67043328
STEP = 8
MESH = pl.DeviceIdType.MESH


def by_core(core, even, odd):
    return even + core * (odd - even)


def weave(first, second):
    return [k for pair in zip(first, second) for k in pair]


def amp_orders(n, mid):
    half, quarter = n // 2, n // 4
    chip = list(range(1, quarter))
    beside = [quarter + a for a in range(quarter)]
    near = [half + quarter * mid + a for a in range(quarter)]
    far = [half + quarter * (1 - mid) + a for a in range(quarter)]
    lead = quarter // 4
    outward = near[:lead] + weave(far, near[lead:]) + far[quarter - lead:]
    outer_order = weave(outward[:quarter], beside) + outward[quarter:] + chip
    middle_rest = beside + [half + a for a in range(quarter)] + chip
    return outer_order, middle_rest


def hole_orders(n, mid):
    half, quarter = n // 2, n // 4
    near = [half + quarter * mid + a for a in reversed(range(quarter))]
    far = [half + quarter * (1 - mid) + a for a in reversed(range(quarter))]
    lead = quarter // 4
    inward = far[:lead] + weave(near, far[lead:]) + near[quarter - lead:]
    staying = [a + b for a in range(quarter) for b in (quarter, 0) if a + b]
    return staying + inward, inward + staying


def residual_kernel(
    n, amps, ladder, chol, pair_ids, occ, vir, result, own_hole,
    amp_own, wide, ladder_v, chol_v, amp_all, hole_all, inverse, vir_v, ids_s, occ_s,
    send_sem, amp_recv, hole_recv, local_sem, entry_sem,
):
    total, rows, width = amps.shape
    pairs = total // n
    full = rows * n
    n_vec = chol.shape[0]
    me = lax.axis_index("pair")
    core = me % 2
    half, quarter = n // 2, n // 4
    mid = (me // quarter + 1) // 2 % 2
    outer_order, middle_rest = amp_orders(n, mid)
    mine = pl.ds(pl.multiple_of(me * rows, rows), rows)
    own_pairs = pl.ds(me * pairs, pairs)

    def rows_of(source):
        return pl.ds(pl.multiple_of(source * rows, rows), rows)

    def amp_copy(k):
        dest = me ^ k
        last = k // half * (k % quarter // (quarter // 2)) * core
        return pltpu.make_async_remote_copy(
            amps.at[pl.ds(dest * pairs, pairs)], amp_all.at[:, mine],
            send_sem.at[0], amp_recv.at[last], device_id={"pair": dest}, device_id_type=MESH,
        )

    def hole_copy(k):
        dest = me ^ k
        cross = k // half
        single = (1 - core) * cross
        slot = single * (k % quarter // 2 * 2 + k // quarter % 2) + (1 - single) * (quarter + 2 * core + cross)
        return pltpu.make_async_remote_copy(
            own_hole.at[pl.ds(dest * pairs, pairs)], hole_all.at[:, mine],
            send_sem.at[1], hole_recv.at[slot], device_id={"pair": dest}, device_id_type=MESH,
        )

    def wait_blocks(ref, count, sem):
        part = ref.at[:, pl.ds(0, count * rows)]
        pltpu.make_async_copy(part, part, sem).wait()

    def wait_sent(ref, sem):
        part = ref.at[pl.ds(0, (n - 1) * pairs)]
        pltpu.make_async_copy(part, part, sem).wait()

    load_amp = pltpu.make_async_copy(amps, amp_own, local_sem.at[0])
    load_ladder = pltpu.make_async_copy(ladder, ladder_v, local_sem.at[1])
    load_chol = pltpu.make_async_copy(chol, chol_v, local_sem.at[2])
    keep_amp = pltpu.make_async_copy(amps.at[own_pairs], amp_all.at[:, mine], local_sem.at[3])
    load_ids = pltpu.make_async_copy(pair_ids, ids_s, local_sem.at[4])
    load_occ = pltpu.make_async_copy(occ, occ_s, local_sem.at[5])
    load_vir = pltpu.make_async_copy(vir, vir_v, local_sem.at[6])

    def tell(sem, k):
        pl.semaphore_signal(sem, inc=1, device_id={"pair": me ^ k}, device_id_type=MESH)

    barrier = pltpu.get_barrier_semaphore()
    low_bits = [1 << i for i in range(quarter.bit_length() - 1)]
    across, along, last = range(len(low_bits), len(low_bits) + 3)

    @pl.when(mid == 1)
    def _():
        tell(barrier, half + quarter)

    for k in low_bits:
        tell(barrier, k)

    @pl.when(mid == 1)
    def _():
        tell(barrier, quarter)

    pl.semaphore_wait(barrier, len(low_bits) + 1)

    def start_near(first, last):
        @pl.when(mid == 1)
        def _():
            for a in range(first, last):
                amp_copy(half + quarter + a).start()

    start_near(0, 1)
    for i, k in enumerate(low_bits):
        tell(entry_sem.at[i], k)
        pl.semaphore_wait(entry_sem.at[i], 1)
        start_near(k, 2 * k)

    @pl.when(mid == 1)
    def _():
        tell(entry_sem.at[across], half + quarter)
        pl.semaphore_wait(entry_sem.at[across], 2)
        tell(entry_sem.at[along], half + quarter)
        tell(entry_sem.at[along], quarter)
        pl.semaphore_wait(entry_sem.at[along], 1)
        tell(entry_sem.at[last], quarter)

    @pl.when(mid == 0)
    def _():
        tell(entry_sem.at[across], quarter)
        pl.semaphore_wait(entry_sem.at[along], 1)
        pl.semaphore_wait(entry_sem.at[last], 1)

    @pl.when(mid == 1)
    def _():
        for k in middle_rest:
            amp_copy(k).start()

    @pl.when(mid == 0)
    def _():
        for k in outer_order:
            amp_copy(k).start()

    load_amp.start()
    load_ladder.start()
    load_chol.start()
    keep_amp.start()
    load_ids.start()
    load_occ.start()
    load_vir.start()

    load_amp.wait()
    load_ladder.wait()
    block = 16
    lanes = 128

    def columns(j, carry):
        cols = pl.ds(pl.multiple_of(j * lanes, lanes), lanes)

        def widen(i, c):
            part = amp_own[pl.ds(i * block, block), :, cols].astype(jnp.float32)
            wide[pl.ds(pl.multiple_of(i * block * rows, block * rows), block * rows), :] = part.reshape(block * rows, lanes)
            return c

        lax.fori_loop(0, total // block, widen, 0)

        def one_row(a, c):
            sel = pl.ds(a, total, stride=rows)
            value = wide[sel, :].astype(jnp.bfloat16)
            wide[sel, :] = jnp.dot(ladder_v[...], value, preferred_element_type=jnp.float32)
            return c

        lax.fori_loop(0, rows, one_row, 0)

        def narrow(i, c):
            part = wide[pl.ds(pl.multiple_of(i * block * rows, block * rows), block * rows), :].astype(jnp.bfloat16)
            amp_own[pl.ds(i * block, block), :, cols] = part.reshape(block, rows, lanes)
            return c

        lax.fori_loop(0, total // block, narrow, 0)
        return carry

    lax.fori_loop(0, width // lanes, columns, 0)
    store_hole = pltpu.make_async_copy(amp_own, own_hole, local_sem.at[0])
    store_hole.start()
    store_hole.wait()

    load_ids.wait()
    load_occ.wait()
    load_vir.wait()

    def one_inverse(p, carry):
        pair = ids_s[p]
        shift = occ_s[pair // NO] + occ_s[pair % NO]

        def add_virtuals(i, c):
            at = pl.ds(pl.multiple_of(i * lanes, lanes), lanes)
            row = vir_v[:, at]
            diagonal = lax.broadcasted_iota(jnp.int32, (lanes, lanes), 0) == lax.broadcasted_iota(jnp.int32, (lanes, lanes), 1)
            column = jnp.sum(jnp.where(diagonal, row, 0.0), axis=1, keepdims=True)
            inverse[p, at, :] = 1.0 / (column + vir_v[...] - shift)
            return c

        lax.fori_loop(0, full // lanes, add_virtuals, 0)
        return carry

    lax.fori_loop(0, pairs, one_inverse, 0)

    wait_sent(amps, send_sem.at[0])
    sent = [by_core(core, even, odd) for even, odd in zip(*hole_orders(n, mid))]
    for k in sent[:half - 1]:
        hole_copy(k).start()
    wait_blocks(amp_all, n - 1 - half // 4, amp_recv.at[0])
    for k in sent[half - 1:half - 1 + STEP]:
        hole_copy(k).start()
    wait_blocks(amp_all, half // 4, amp_recv.at[1])
    for k in sent[half - 1 + STEP:]:
        hole_copy(k).start()
    keep_hole = pltpu.make_async_copy(own_hole.at[own_pairs], hole_all.at[:, mine], local_sem.at[1])
    keep_hole.start()

    load_chol.wait()
    keep_amp.wait()

    def one_pair(p, carry):
        result[p] = jnp.zeros((full, full), jnp.float32)

        def one_vector(q, c):
            vector = chol_v[q]
            mixed = jnp.dot(vector, amp_all[p], preferred_element_type=jnp.float32).astype(jnp.bfloat16)
            result[p] += lax.dot_general(
                mixed, vector, (((1,), (1,)), ((), ())), preferred_element_type=jnp.float32
            )
            return c

        lax.fori_loop(0, n_vec, one_vector, 0)
        return carry

    lax.fori_loop(0, pairs, one_pair, 0)

    def finish(k):
        at = rows_of(me ^ k)

        def one(p, carry):
            result[p, at, :] = (hole_all[p, at, :].astype(jnp.float32) + result[p, at, :]) * inverse[p, at, :]
            return carry

        lax.fori_loop(0, pairs, one, 0)

    keep_hole.wait()

    def finish_some(base):
        def one(i, carry):
            finish(base + 2 * i)
            return carry

        lax.fori_loop(0, half // 2, one, 0)

    def wait_staying(slot, fewer):
        @pl.when(fewer == 1)
        def _():
            wait_blocks(hole_all, half // 2 - 1, hole_recv.at[slot])

        @pl.when(fewer == 0)
        def _():
            wait_blocks(hole_all, half // 2, hole_recv.at[slot])

    wait_staying(quarter, 1 - core)
    finish_some(core)
    wait_blocks(hole_all, half // 2, hole_recv.at[quarter + 3])
    finish_some(half + 1 - core)
    wait_staying(quarter + 2, core)
    finish_some(1 - core)
    for a in reversed(range(quarter // 2)):
        for step in range(2):
            wait_blocks(hole_all, 1, hole_recv.at[2 * a + step])
            finish(half + quarter * step + 2 * a + core)
    wait_sent(own_hole, send_sem.at[1])


def write_kernel(result, out, sems):
    pieces = sems.shape[0]
    size = result.shape[0] // pieces
    puts = [
        pltpu.make_async_copy(result.at[pl.ds(i * size, size)], out.at[pl.ds(i * size, size)], sems.at[i])
        for i in range(pieces)
    ]
    for put in puts:
        put.start()
    for put in puts:
        put.wait()


def exchange_and_contract(amplitudes, ladder, cholesky, pair_ids, occ_energy, vir_energy):
    n = lax.axis_size("pair")
    total, rows, width = amplitudes.shape
    pairs = total // n
    full = rows * n
    anywhere = pl.BlockSpec(memory_space=pl.ANY)
    in_hbm = pl.BlockSpec(memory_space=pltpu.HBM)
    in_vmem = pl.BlockSpec(memory_space=pltpu.VMEM)
    result, _ = pl.pallas_call(
        functools.partial(residual_kernel, n),
        out_shape=[
            pltpu.VMEM((pairs, full, full), jnp.float32),
            jax.ShapeDtypeStruct(amplitudes.shape, jnp.bfloat16),
        ],
        in_specs=[in_hbm] * 6,
        out_specs=[in_vmem, in_hbm],
        scratch_shapes=[
            pltpu.VMEM(amplitudes.shape, jnp.bfloat16),
            pltpu.VMEM((total * rows, 128), jnp.float32),
            pltpu.VMEM(ladder.shape, jnp.bfloat16),
            pltpu.VMEM(cholesky.shape, jnp.bfloat16),
            pltpu.VMEM((pairs, full, width), jnp.bfloat16),
            pltpu.VMEM((pairs, full, width), jnp.bfloat16),
            pltpu.VMEM((pairs, full, full), jnp.float32),
            pltpu.VMEM((1, full), jnp.float32),
            pltpu.SMEM(pair_ids.shape, jnp.int32),
            pltpu.SMEM(occ_energy.shape, jnp.float32),
            pltpu.SemaphoreType.DMA((2,)),
            pltpu.SemaphoreType.DMA((2,)),
            pltpu.SemaphoreType.DMA((n // 4 + 4,)),
            pltpu.SemaphoreType.DMA((7,)),
            pltpu.SemaphoreType.REGULAR((n.bit_length(),)),
        ],
        compiler_params=pltpu.CompilerParams(
            collective_id=0, has_side_effects=True, vmem_limit_bytes=VMEM_BYTES - 4 * pairs * full * full
        ),
    )(amplitudes, ladder, cholesky, pair_ids, occ_energy, vir_energy.reshape(1, -1))
    return pl.pallas_call(
        write_kernel,
        out_shape=jax.ShapeDtypeStruct((pairs, full, full), jnp.float32),
        in_specs=[in_vmem],
        out_specs=in_hbm,
        scratch_shapes=[pltpu.SemaphoreType.DMA((1,))],
        compiler_params=pltpu.CompilerParams(vmem_limit_bytes=8 * 1024 * 1024),
    )(result)


def exchange_plain(amplitudes, ladder, cholesky):
    flat = amplitudes.reshape(amplitudes.shape[0], -1)
    hole = jnp.dot(ladder, flat, preferred_element_type=jnp.float32).astype(jnp.bfloat16)
    hole = hole.reshape(amplitudes.shape)
    pair_amps = lax.all_to_all(amplitudes, "pair", split_axis=0, concat_axis=1, tiled=True)
    pair_hole = lax.all_to_all(hole, "pair", split_axis=0, concat_axis=1, tiled=True)
    mixed = jnp.einsum(
        "qac,pcd->qpad", cholesky, pair_amps, preferred_element_type=jnp.float32
    ).astype(jnp.bfloat16)
    particle = jnp.einsum("qpad,qbd->pab", mixed, cholesky, preferred_element_type=jnp.float32)
    return pair_hole, particle


def shards(amplitudes, ladder, cholesky, pair_ids, occ_energy, vir_energy):
    n = lax.axis_size("pair")
    n_aux = lax.axis_size("aux")
    half_width = amplitudes.shape[2] // n_aux
    aux_index = lax.axis_index("aux")
    aligned = amplitudes.shape[1] % 16 == 0 and n & (n - 1) == 0 and n >= 16
    if aligned and n_aux == 1:
        return exchange_and_contract(amplitudes, ladder, cholesky, pair_ids, occ_energy, vir_energy)
    hole, particle = exchange_plain(amplitudes, ladder, cholesky)
    if n_aux > 1:
        hole = lax.dynamic_slice_in_dim(hole, aux_index * half_width, half_width, 2)
        particle = lax.psum_scatter(particle, "aux", scatter_dimension=2, tiled=True)
    orbitals = jnp.arange(NO, dtype=jnp.int32)
    first_hot = (pair_ids // NO)[:, None] == orbitals[None, :]
    second_hot = (pair_ids % NO)[:, None] == orbitals[None, :]
    hot = first_hot.astype(jnp.float32) + second_hot.astype(jnp.float32)
    occ_sum = jnp.sum(hot * occ_energy[None, :], axis=1)
    vir_cols = lax.dynamic_slice_in_dim(vir_energy, aux_index * half_width, half_width, 0)
    denominator = vir_energy[None, :, None] + vir_cols[None, None, :] - occ_sum[:, None, None]
    return (hole.astype(jnp.float32) + particle) / denominator


def solution(mesh):
    in_specs = (P(None, "pair", None), P(), P("aux", None, None), P("pair"), P(), P())
    out_specs = P("pair", None, "aux")
    return jax.shard_map(shards, mesh=mesh, in_specs=in_specs, out_specs=out_specs, check_vma=False)
```

```python
import functools

import jax
import jax.numpy as jnp
from jax import lax
from jax.experimental import pallas as pl
from jax.experimental.pallas import tpu as pltpu
from jax.sharding import PartitionSpec as P

NO = 16
VMEM_BYTES = 67043328
STEP = 8
MESH = pl.DeviceIdType.MESH


def by_core(core, even, odd):
    return even + core * (odd - even)


def weave(first, second):
    return [k for pair in zip(first, second) for k in pair]


def amp_orders(n, mid):
    half, quarter = n // 2, n // 4
    chip = list(range(1, quarter))
    beside = [quarter + a for a in range(quarter)]
    near = [half + quarter * mid + a for a in range(quarter)]
    far = [half + quarter * (1 - mid) + a for a in range(quarter)]
    lead = quarter // 4
    outward = near[:lead] + weave(far, near[lead:]) + far[quarter - lead:]
    outer_order = weave(outward[:quarter], beside) + outward[quarter:] + chip
    middle_rest = beside + [half + a for a in range(quarter)] + chip
    return outer_order, middle_rest


def hole_orders(n, mid):
    half, quarter = n // 2, n // 4
    near = [half + quarter * mid + a for a in reversed(range(quarter))]
    far = [half + quarter * (1 - mid) + a for a in reversed(range(quarter))]
    lead = quarter // 4
    inward = far[:lead] + weave(near, far[lead:]) + near[quarter - lead:]
    inward[-1], inward[-2] = inward[-2], inward[-1]
    staying = [a + b for a in range(quarter) for b in (quarter, 0) if a + b]
    return staying + inward, inward + staying


def residual_kernel(
    n, amps, ladder, chol, pair_ids, occ, vir, result, own_hole,
    amp_own, wide, ladder_v, chol_v, amp_all, hole_all, inverse, vir_v, ids_s, occ_s,
    send_sem, amp_recv, hole_recv, local_sem, entry_sem,
):
    total, rows, width = amps.shape
    pairs = total // n
    full = rows * n
    n_vec = chol.shape[0]
    me = lax.axis_index("pair")
    core = me % 2
    half, quarter = n // 2, n // 4
    mid = (me // quarter + 1) // 2 % 2
    outer_order, middle_rest = amp_orders(n, mid)
    mine = pl.ds(pl.multiple_of(me * rows, rows), rows)
    own_pairs = pl.ds(me * pairs, pairs)

    def rows_of(source):
        return pl.ds(pl.multiple_of(source * rows, rows), rows)

    def amp_copy(k):
        dest = me ^ k
        last = k // half * (k % quarter // (quarter // 2)) * core
        return pltpu.make_async_remote_copy(
            amps.at[pl.ds(dest * pairs, pairs)], amp_all.at[:, mine],
            send_sem.at[0], amp_recv.at[last], device_id={"pair": dest}, device_id_type=MESH,
        )

    def hole_copy(k):
        dest = me ^ k
        cross = k // half
        single = (1 - core) * cross
        slot = single * (k % quarter // 2 * 2 + k // quarter % 2) + (1 - single) * (quarter + 2 * core + cross)
        return pltpu.make_async_remote_copy(
            own_hole.at[pl.ds(dest * pairs, pairs)], hole_all.at[:, mine],
            send_sem.at[1], hole_recv.at[slot], device_id={"pair": dest}, device_id_type=MESH,
        )

    def wait_blocks(ref, count, sem):
        part = ref.at[:, pl.ds(0, count * rows)]
        pltpu.make_async_copy(part, part, sem).wait()

    def wait_sent(ref, sem):
        part = ref.at[pl.ds(0, (n - 1) * pairs)]
        pltpu.make_async_copy(part, part, sem).wait()

    load_amp = pltpu.make_async_copy(amps, amp_own, local_sem.at[0])
    load_ladder = pltpu.make_async_copy(ladder, ladder_v, local_sem.at[1])
    load_chol = pltpu.make_async_copy(chol, chol_v, local_sem.at[2])
    keep_amp = pltpu.make_async_copy(amps.at[own_pairs], amp_all.at[:, mine], local_sem.at[3])
    load_ids = pltpu.make_async_copy(pair_ids, ids_s, local_sem.at[4])
    load_occ = pltpu.make_async_copy(occ, occ_s, local_sem.at[5])
    load_vir = pltpu.make_async_copy(vir, vir_v, local_sem.at[6])

    def tell(sem, k):
        pl.semaphore_signal(sem, inc=1, device_id={"pair": me ^ k}, device_id_type=MESH)

    barrier = pltpu.get_barrier_semaphore()
    low_bits = [1 << i for i in range(quarter.bit_length() - 1)]
    across, along, last = range(len(low_bits), len(low_bits) + 3)

    @pl.when(mid == 1)
    def _():
        tell(barrier, half + quarter)

    for k in low_bits:
        tell(barrier, k)

    @pl.when(mid == 1)
    def _():
        tell(barrier, quarter)

    load_amp.start()
    load_ladder.start()
    load_chol.start()
    keep_amp.start()
    load_ids.start()
    load_occ.start()
    load_vir.start()

    pl.semaphore_wait(barrier, len(low_bits) + 1)

    def start_near(first, last):
        @pl.when(mid == 1)
        def _():
            for a in range(first, last):
                amp_copy(half + quarter + a).start()

    start_near(0, 1)
    for i, k in enumerate(low_bits):
        tell(entry_sem.at[i], k)
        pl.semaphore_wait(entry_sem.at[i], 1)
        start_near(k, 2 * k)

    @pl.when(mid == 1)
    def _():
        tell(entry_sem.at[across], half + quarter)
        pl.semaphore_wait(entry_sem.at[across], 2)
        tell(entry_sem.at[along], half + quarter)
        tell(entry_sem.at[along], quarter)
        pl.semaphore_wait(entry_sem.at[along], 1)
        tell(entry_sem.at[last], quarter)

    @pl.when(mid == 0)
    def _():
        tell(entry_sem.at[across], quarter)
        pl.semaphore_wait(entry_sem.at[along], 1)
        pl.semaphore_wait(entry_sem.at[last], 1)

    @pl.when(mid == 1)
    def _():
        for k in middle_rest:
            amp_copy(k).start()

    @pl.when(mid == 0)
    def _():
        for k in outer_order:
            amp_copy(k).start()

    load_amp.wait()
    load_ladder.wait()
    block = 16
    lanes = 128

    def columns(j, carry):
        cols = pl.ds(pl.multiple_of(j * lanes, lanes), lanes)

        def widen(i, c):
            part = amp_own[pl.ds(i * block, block), :, cols].astype(jnp.float32)
            wide[pl.ds(pl.multiple_of(i * block * rows, block * rows), block * rows), :] = part.reshape(block * rows, lanes)
            return c

        lax.fori_loop(0, total // block, widen, 0)

        def one_row(a, c):
            sel = pl.ds(a, total, stride=rows)
            value = wide[sel, :].astype(jnp.bfloat16)
            wide[sel, :] = jnp.dot(ladder_v[...], value, preferred_element_type=jnp.float32)
            return c

        lax.fori_loop(0, rows, one_row, 0)

        def narrow(i, c):
            part = wide[pl.ds(pl.multiple_of(i * block * rows, block * rows), block * rows), :].astype(jnp.bfloat16)
            amp_own[pl.ds(i * block, block), :, cols] = part.reshape(block, rows, lanes)
            return c

        lax.fori_loop(0, total // block, narrow, 0)
        return carry

    lax.fori_loop(0, width // lanes, columns, 0)
    store_hole = pltpu.make_async_copy(amp_own, own_hole, local_sem.at[0])
    store_hole.start()
    store_hole.wait()

    load_ids.wait()
    load_occ.wait()
    load_vir.wait()

    def one_inverse(p, carry):
        pair = ids_s[p]
        shift = occ_s[pair // NO] + occ_s[pair % NO]

        def add_virtuals(i, c):
            at = pl.ds(pl.multiple_of(i * lanes, lanes), lanes)
            row = vir_v[:, at]
            diagonal = lax.broadcasted_iota(jnp.int32, (lanes, lanes), 0) == lax.broadcasted_iota(jnp.int32, (lanes, lanes), 1)
            column = jnp.sum(jnp.where(diagonal, row, 0.0), axis=1, keepdims=True)
            inverse[p, at, :] = 1.0 / (column + vir_v[...] - shift)
            return c

        lax.fori_loop(0, full // lanes, add_virtuals, 0)
        return carry

    lax.fori_loop(0, pairs, one_inverse, 0)

    wait_sent(amps, send_sem.at[0])
    sent = [by_core(core, even, odd) for even, odd in zip(*hole_orders(n, mid))]
    for k in sent[:half - 1]:
        hole_copy(k).start()
    wait_blocks(amp_all, n - 1 - half // 4, amp_recv.at[0])
    for k in sent[half - 1:half - 1 + STEP]:
        hole_copy(k).start()
    wait_blocks(amp_all, half // 4, amp_recv.at[1])
    for k in sent[half - 1 + STEP:]:
        hole_copy(k).start()
    keep_hole = pltpu.make_async_copy(own_hole.at[own_pairs], hole_all.at[:, mine], local_sem.at[1])
    keep_hole.start()

    load_chol.wait()
    keep_amp.wait()

    def one_pair(p, carry):
        result[p] = jnp.zeros((full, full), jnp.float32)

        def one_vector(q, c):
            vector = chol_v[q]
            mixed = jnp.dot(vector, amp_all[p], preferred_element_type=jnp.float32).astype(jnp.bfloat16)
            result[p] += lax.dot_general(
                mixed, vector, (((1,), (1,)), ((), ())), preferred_element_type=jnp.float32
            )
            return c

        lax.fori_loop(0, n_vec, one_vector, 0)
        return carry

    lax.fori_loop(0, pairs, one_pair, 0)

    def finish(k):
        at = rows_of(me ^ k)

        def one(p, carry):
            result[p, at, :] = (hole_all[p, at, :].astype(jnp.float32) + result[p, at, :]) * inverse[p, at, :]
            return carry

        lax.fori_loop(0, pairs, one, 0)

    keep_hole.wait()

    def finish_some(base):
        def one(i, carry):
            finish(base + 2 * i)
            return carry

        lax.fori_loop(0, half // 2, one, 0)

    def wait_staying(slot, fewer):
        @pl.when(fewer == 1)
        def _():
            wait_blocks(hole_all, half // 2 - 1, hole_recv.at[slot])

        @pl.when(fewer == 0)
        def _():
            wait_blocks(hole_all, half // 2, hole_recv.at[slot])

    wait_staying(quarter, 1 - core)
    finish_some(core)
    wait_blocks(hole_all, half // 2, hole_recv.at[quarter + 3])
    finish_some(half + 1 - core)
    wait_staying(quarter + 2, core)
    finish_some(1 - core)
    for a in reversed(range(quarter // 2)):
        for step in range(2):
            wait_blocks(hole_all, 1, hole_recv.at[2 * a + step])
            finish(half + quarter * step + 2 * a + core)
    wait_sent(own_hole, send_sem.at[1])


def write_kernel(result, out, sems):
    pieces = sems.shape[0]
    size = result.shape[0] // pieces
    puts = [
        pltpu.make_async_copy(result.at[pl.ds(i * size, size)], out.at[pl.ds(i * size, size)], sems.at[i])
        for i in range(pieces)
    ]
    for put in puts:
        put.start()
    for put in puts:
        put.wait()


def exchange_and_contract(amplitudes, ladder, cholesky, pair_ids, occ_energy, vir_energy):
    n = lax.axis_size("pair")
    total, rows, width = amplitudes.shape
    pairs = total // n
    full = rows * n
    anywhere = pl.BlockSpec(memory_space=pl.ANY)
    in_hbm = pl.BlockSpec(memory_space=pltpu.HBM)
    in_vmem = pl.BlockSpec(memory_space=pltpu.VMEM)
    result, _ = pl.pallas_call(
        functools.partial(residual_kernel, n),
        out_shape=[
            pltpu.VMEM((pairs, full, full), jnp.float32),
            jax.ShapeDtypeStruct(amplitudes.shape, jnp.bfloat16),
        ],
        in_specs=[in_hbm] * 6,
        out_specs=[in_vmem, in_hbm],
        scratch_shapes=[
            pltpu.VMEM(amplitudes.shape, jnp.bfloat16),
            pltpu.VMEM((total * rows, 128), jnp.float32),
            pltpu.VMEM(ladder.shape, jnp.bfloat16),
            pltpu.VMEM(cholesky.shape, jnp.bfloat16),
            pltpu.VMEM((pairs, full, width), jnp.bfloat16),
            pltpu.VMEM((pairs, full, width), jnp.bfloat16),
            pltpu.VMEM((pairs, full, full), jnp.float32),
            pltpu.VMEM((1, full), jnp.float32),
            pltpu.SMEM(pair_ids.shape, jnp.int32),
            pltpu.SMEM(occ_energy.shape, jnp.float32),
            pltpu.SemaphoreType.DMA((2,)),
            pltpu.SemaphoreType.DMA((2,)),
            pltpu.SemaphoreType.DMA((n // 4 + 4,)),
            pltpu.SemaphoreType.DMA((7,)),
            pltpu.SemaphoreType.REGULAR((n.bit_length(),)),
        ],
        compiler_params=pltpu.CompilerParams(
            collective_id=0, has_side_effects=True, vmem_limit_bytes=VMEM_BYTES - 4 * pairs * full * full
        ),
    )(amplitudes, ladder, cholesky, pair_ids, occ_energy, vir_energy.reshape(1, -1))
    return pl.pallas_call(
        write_kernel,
        out_shape=jax.ShapeDtypeStruct((pairs, full, full), jnp.float32),
        in_specs=[in_vmem],
        out_specs=in_hbm,
        scratch_shapes=[pltpu.SemaphoreType.DMA((pairs,))],
        compiler_params=pltpu.CompilerParams(vmem_limit_bytes=8 * 1024 * 1024),
    )(result)


def exchange_plain(amplitudes, ladder, cholesky):
    flat = amplitudes.reshape(amplitudes.shape[0], -1)
    hole = jnp.dot(ladder, flat, preferred_element_type=jnp.float32).astype(jnp.bfloat16)
    hole = hole.reshape(amplitudes.shape)
    pair_amps = lax.all_to_all(amplitudes, "pair", split_axis=0, concat_axis=1, tiled=True)
    pair_hole = lax.all_to_all(hole, "pair", split_axis=0, concat_axis=1, tiled=True)
    mixed = jnp.einsum(
        "qac,pcd->qpad", cholesky, pair_amps, preferred_element_type=jnp.float32
    ).astype(jnp.bfloat16)
    particle = jnp.einsum("qpad,qbd->pab", mixed, cholesky, preferred_element_type=jnp.float32)
    return pair_hole, particle


def shards(amplitudes, ladder, cholesky, pair_ids, occ_energy, vir_energy):
    n = lax.axis_size("pair")
    n_aux = lax.axis_size("aux")
    half_width = amplitudes.shape[2] // n_aux
    aux_index = lax.axis_index("aux")
    aligned = amplitudes.shape[1] % 16 == 0 and n & (n - 1) == 0 and n >= 16
    if aligned and n_aux == 1:
        return exchange_and_contract(amplitudes, ladder, cholesky, pair_ids, occ_energy, vir_energy)
    hole, particle = exchange_plain(amplitudes, ladder, cholesky)
    if n_aux > 1:
        hole = lax.dynamic_slice_in_dim(hole, aux_index * half_width, half_width, 2)
        particle = lax.psum_scatter(particle, "aux", scatter_dimension=2, tiled=True)
    orbitals = jnp.arange(NO, dtype=jnp.int32)
    first_hot = (pair_ids // NO)[:, None] == orbitals[None, :]
    second_hot = (pair_ids % NO)[:, None] == orbitals[None, :]
    hot = first_hot.astype(jnp.float32) + second_hot.astype(jnp.float32)
    occ_sum = jnp.sum(hot * occ_energy[None, :], axis=1)
    vir_cols = lax.dynamic_slice_in_dim(vir_energy, aux_index * half_width, half_width, 0)
    denominator = vir_energy[None, :, None] + vir_cols[None, None, :] - occ_sum[:, None, None]
    return (hole.astype(jnp.float32) + particle) / denominator


def solution(mesh):
    in_specs = (P(None, "pair", None), P(), P("aux", None, None), P("pair"), P(), P())
    out_specs = P("pair", None, "aux")
    return jax.shard_map(shards, mesh=mesh, in_specs=in_specs, out_specs=out_specs, check_vma=False)
```

```python
import functools

import jax
import jax.numpy as jnp
from jax import lax
from jax.experimental import pallas as pl
from jax.experimental.pallas import tpu as pltpu
from jax.sharding import PartitionSpec as P

NO = 16
VMEM_BYTES = 67043328
STEP = 8
MESH = pl.DeviceIdType.MESH


def by_core(core, even, odd):
    return even + core * (odd - even)


def weave(first, second):
    return [k for pair in zip(first, second) for k in pair]


def amp_orders(n, mid):
    half, quarter = n // 2, n // 4
    chip = list(range(1, quarter))
    beside = [quarter + a for a in range(quarter)]
    near = [half + quarter * mid + a for a in range(quarter)]
    far = [half + quarter * (1 - mid) + a for a in range(quarter)]
    lead = quarter // 4
    outward = near[:lead] + weave(far, near[lead:]) + far[quarter - lead:]
    outer_order = weave(outward[:quarter], beside) + outward[quarter:] + chip
    middle_rest = beside + [half + a for a in range(quarter)] + chip
    return outer_order, middle_rest


def hole_orders(n, mid):
    half, quarter = n // 2, n // 4
    near = [half + quarter * mid + a for a in reversed(range(quarter))]
    far = [half + quarter * (1 - mid) + a for a in reversed(range(quarter))]
    lead = quarter // 4
    inward = far[:lead] + weave(near, far[lead:]) + near[quarter - lead:]
    staying = [a + b for a in range(quarter) for b in (quarter, 0) if a + b]
    return staying + inward, inward + staying


def residual_kernel(
    n, amps, ladder, chol, pair_ids, occ, vir, result, own_hole,
    amp_own, wide, ladder_v, chol_v, amp_all, hole_all, inverse, vir_v, ids_s, occ_s,
    send_sem, amp_recv, hole_recv, local_sem, entry_sem,
):
    total, rows, width = amps.shape
    pairs = total // n
    full = rows * n
    n_vec = chol.shape[0]
    me = lax.axis_index("pair")
    core = me % 2
    half, quarter = n // 2, n // 4
    mid = (me // quarter + 1) // 2 % 2
    outer_order, middle_rest = amp_orders(n, mid)
    mine = pl.ds(pl.multiple_of(me * rows, rows), rows)
    own_pairs = pl.ds(me * pairs, pairs)

    def rows_of(source):
        return pl.ds(pl.multiple_of(source * rows, rows), rows)

    def amp_copy(k):
        dest = me ^ k
        last = k // half * (k % quarter // (quarter // 2)) * core
        return pltpu.make_async_remote_copy(
            amps.at[pl.ds(dest * pairs, pairs)], amp_all.at[:, mine],
            send_sem.at[0], amp_recv.at[last], device_id={"pair": dest}, device_id_type=MESH,
        )

    def hole_copy(k):
        dest = me ^ k
        cross = k // half
        single = (1 - core) * cross
        slot = single * (k % quarter // 2 * 2 + k // quarter % 2) + (1 - single) * (quarter + 2 * core + cross)
        return pltpu.make_async_remote_copy(
            own_hole.at[pl.ds(dest * pairs, pairs)], hole_all.at[:, mine],
            send_sem.at[1], hole_recv.at[slot], device_id={"pair": dest}, device_id_type=MESH,
        )

    def wait_blocks(ref, count, sem):
        part = ref.at[:, pl.ds(0, count * rows)]
        pltpu.make_async_copy(part, part, sem).wait()

    def wait_sent(ref, sem):
        part = ref.at[pl.ds(0, (n - 1) * pairs)]
        pltpu.make_async_copy(part, part, sem).wait()

    load_amp = pltpu.make_async_copy(amps, amp_own, local_sem.at[0])
    load_ladder = pltpu.make_async_copy(ladder, ladder_v, local_sem.at[1])
    load_chol = pltpu.make_async_copy(chol, chol_v, local_sem.at[2])
    keep_amp = pltpu.make_async_copy(amps.at[own_pairs], amp_all.at[:, mine], local_sem.at[3])
    load_ids = pltpu.make_async_copy(pair_ids, ids_s, local_sem.at[4])
    load_occ = pltpu.make_async_copy(occ, occ_s, local_sem.at[5])
    load_vir = pltpu.make_async_copy(vir, vir_v, local_sem.at[6])

    def tell(sem, k):
        pl.semaphore_signal(sem, inc=1, device_id={"pair": me ^ k}, device_id_type=MESH)

    barrier = pltpu.get_barrier_semaphore()
    low_bits = [1 << i for i in range(quarter.bit_length() - 1)]
    across, along, last = range(len(low_bits), len(low_bits) + 3)

    @pl.when(mid == 1)
    def _():
        tell(barrier, half + quarter)

    for k in low_bits:
        tell(barrier, k)

    @pl.when(mid == 1)
    def _():
        tell(barrier, quarter)

    load_amp.start()
    load_ladder.start()
    load_chol.start()
    keep_amp.start()
    load_ids.start()
    load_occ.start()
    load_vir.start()

    pl.semaphore_wait(barrier, len(low_bits) + 1)

    def start_near(first, last):
        @pl.when(mid == 1)
        def _():
            for a in range(first, last):
                amp_copy(half + quarter + a).start()

    start_near(0, 1)
    for i, k in enumerate(low_bits):
        tell(entry_sem.at[i], k)
        pl.semaphore_wait(entry_sem.at[i], 1)
        start_near(k, 2 * k)

    @pl.when(mid == 1)
    def _():
        tell(entry_sem.at[across], half + quarter)
        pl.semaphore_wait(entry_sem.at[across], 2)
        tell(entry_sem.at[along], half + quarter)
        tell(entry_sem.at[along], quarter)
        pl.semaphore_wait(entry_sem.at[along], 1)
        tell(entry_sem.at[last], quarter)

    @pl.when(mid == 0)
    def _():
        tell(entry_sem.at[across], quarter)
        pl.semaphore_wait(entry_sem.at[along], 1)
        pl.semaphore_wait(entry_sem.at[last], 1)

    @pl.when(mid == 1)
    def _():
        for k in middle_rest:
            amp_copy(k).start()

    @pl.when(mid == 0)
    def _():
        for k in outer_order:
            amp_copy(k).start()

    load_amp.wait()
    load_ladder.wait()
    block = 16
    lanes = 128

    def columns(j, carry):
        cols = pl.ds(pl.multiple_of(j * lanes, lanes), lanes)

        def widen(i, c):
            part = amp_own[pl.ds(i * block, block), :, cols].astype(jnp.float32)
            wide[pl.ds(pl.multiple_of(i * block * rows, block * rows), block * rows), :] = part.reshape(block * rows, lanes)
            return c

        lax.fori_loop(0, total // block, widen, 0)

        def one_row(a, c):
            sel = pl.ds(a, total, stride=rows)
            value = wide[sel, :].astype(jnp.bfloat16)
            wide[sel, :] = jnp.dot(ladder_v[...], value, preferred_element_type=jnp.float32)
            return c

        lax.fori_loop(0, rows, one_row, 0)

        def narrow(i, c):
            part = wide[pl.ds(pl.multiple_of(i * block * rows, block * rows), block * rows), :].astype(jnp.bfloat16)
            amp_own[pl.ds(i * block, block), :, cols] = part.reshape(block, rows, lanes)
            return c

        lax.fori_loop(0, total // block, narrow, 0)
        return carry

    lax.fori_loop(0, width // lanes, columns, 0)
    store_hole = pltpu.make_async_copy(amp_own, own_hole, local_sem.at[0])
    store_hole.start()
    store_hole.wait()

    load_ids.wait()
    load_occ.wait()
    load_vir.wait()

    def one_inverse(p, carry):
        pair = ids_s[p]
        shift = occ_s[pair // NO] + occ_s[pair % NO]

        def add_virtuals(i, c):
            at = pl.ds(pl.multiple_of(i * lanes, lanes), lanes)
            row = vir_v[:, at]
            diagonal = lax.broadcasted_iota(jnp.int32, (lanes, lanes), 0) == lax.broadcasted_iota(jnp.int32, (lanes, lanes), 1)
            column = jnp.sum(jnp.where(diagonal, row, 0.0), axis=1, keepdims=True)
            inverse[p, at, :] = 1.0 / (column + vir_v[...] - shift)
            return c

        lax.fori_loop(0, full // lanes, add_virtuals, 0)
        return carry

    lax.fori_loop(0, pairs, one_inverse, 0)

    wait_sent(amps, send_sem.at[0])
    sent = [by_core(core, even, odd) for even, odd in zip(*hole_orders(n, mid))]
    for k in sent[:half - 1]:
        hole_copy(k).start()
    wait_blocks(amp_all, n - 1 - half // 4, amp_recv.at[0])
    for k in sent[half - 1:half - 1 + STEP]:
        hole_copy(k).start()
    wait_blocks(amp_all, half // 4, amp_recv.at[1])
    for k in sent[half - 1 + STEP:]:
        hole_copy(k).start()
    keep_hole = pltpu.make_async_copy(own_hole.at[own_pairs], hole_all.at[:, mine], local_sem.at[1])
    keep_hole.start()

    load_chol.wait()
    keep_amp.wait()

    def one_pair(p, carry):
        result[p] = jnp.zeros((full, full), jnp.float32)

        def one_vector(q, c):
            vector = chol_v[q]
            mixed = jnp.dot(vector, amp_all[p], preferred_element_type=jnp.float32).astype(jnp.bfloat16)
            result[p] += lax.dot_general(
                mixed, vector, (((1,), (1,)), ((), ())), preferred_element_type=jnp.float32
            )
            return c

        lax.fori_loop(0, n_vec, one_vector, 0)
        return carry

    lax.fori_loop(0, pairs, one_pair, 0)

    def finish(k):
        at = rows_of(me ^ k)

        def one(p, carry):
            result[p, at, :] = (hole_all[p, at, :].astype(jnp.float32) + result[p, at, :]) * inverse[p, at, :]
            return carry

        lax.fori_loop(0, pairs, one, 0)

    keep_hole.wait()

    def finish_some(base):
        def one(i, carry):
            finish(base + 2 * i)
            return carry

        lax.fori_loop(0, half // 2, one, 0)

    def wait_staying(slot, fewer):
        @pl.when(fewer == 1)
        def _():
            wait_blocks(hole_all, half // 2 - 1, hole_recv.at[slot])

        @pl.when(fewer == 0)
        def _():
            wait_blocks(hole_all, half // 2, hole_recv.at[slot])

    wait_staying(quarter, 1 - core)
    finish_some(core)
    wait_blocks(hole_all, half // 2, hole_recv.at[quarter + 3])
    finish_some(half + 1 - core)
    wait_staying(quarter + 2, core)
    finish_some(1 - core)
    for a in reversed(range(quarter // 2)):
        for step in range(2):
            wait_blocks(hole_all, 1, hole_recv.at[2 * a + step])
            finish(half + quarter * step + 2 * a + core)
    wait_sent(own_hole, send_sem.at[1])


def exchange_and_contract(amplitudes, ladder, cholesky, pair_ids, occ_energy, vir_energy):
    n = lax.axis_size("pair")
    total, rows, width = amplitudes.shape
    pairs = total // n
    full = rows * n
    anywhere = pl.BlockSpec(memory_space=pl.ANY)
    in_hbm = pl.BlockSpec(memory_space=pltpu.HBM)
    in_vmem = pl.BlockSpec(memory_space=pltpu.VMEM)
    result, _ = pl.pallas_call(
        functools.partial(residual_kernel, n),
        out_shape=[
            pltpu.VMEM((pairs, full, full), jnp.float32),
            jax.ShapeDtypeStruct(amplitudes.shape, jnp.bfloat16),
        ],
        in_specs=[in_hbm] * 6,
        out_specs=[in_vmem, in_hbm],
        scratch_shapes=[
            pltpu.VMEM(amplitudes.shape, jnp.bfloat16),
            pltpu.VMEM((total * rows, 128), jnp.float32),
            pltpu.VMEM(ladder.shape, jnp.bfloat16),
            pltpu.VMEM(cholesky.shape, jnp.bfloat16),
            pltpu.VMEM((pairs, full, width), jnp.bfloat16),
            pltpu.VMEM((pairs, full, width), jnp.bfloat16),
            pltpu.VMEM((pairs, full, full), jnp.float32),
            pltpu.VMEM((1, full), jnp.float32),
            pltpu.SMEM(pair_ids.shape, jnp.int32),
            pltpu.SMEM(occ_energy.shape, jnp.float32),
            pltpu.SemaphoreType.DMA((2,)),
            pltpu.SemaphoreType.DMA((2,)),
            pltpu.SemaphoreType.DMA((n // 4 + 4,)),
            pltpu.SemaphoreType.DMA((7,)),
            pltpu.SemaphoreType.REGULAR((n.bit_length(),)),
        ],
        compiler_params=pltpu.CompilerParams(
            collective_id=0, has_side_effects=True, vmem_limit_bytes=VMEM_BYTES - 4 * pairs * full * full
        ),
    )(amplitudes, ladder, cholesky, pair_ids, occ_energy, vir_energy.reshape(1, -1))
    return result


def exchange_plain(amplitudes, ladder, cholesky):
    flat = amplitudes.reshape(amplitudes.shape[0], -1)
    hole = jnp.dot(ladder, flat, preferred_element_type=jnp.float32).astype(jnp.bfloat16)
    hole = hole.reshape(amplitudes.shape)
    pair_amps = lax.all_to_all(amplitudes, "pair", split_axis=0, concat_axis=1, tiled=True)
    pair_hole = lax.all_to_all(hole, "pair", split_axis=0, concat_axis=1, tiled=True)
    mixed = jnp.einsum(
        "qac,pcd->qpad", cholesky, pair_amps, preferred_element_type=jnp.float32
    ).astype(jnp.bfloat16)
    particle = jnp.einsum("qpad,qbd->pab", mixed, cholesky, preferred_element_type=jnp.float32)
    return pair_hole, particle


def shards(amplitudes, ladder, cholesky, pair_ids, occ_energy, vir_energy):
    n = lax.axis_size("pair")
    n_aux = lax.axis_size("aux")
    half_width = amplitudes.shape[2] // n_aux
    aux_index = lax.axis_index("aux")
    aligned = amplitudes.shape[1] % 16 == 0 and n & (n - 1) == 0 and n >= 16
    if aligned and n_aux == 1:
        return exchange_and_contract(amplitudes, ladder, cholesky, pair_ids, occ_energy, vir_energy)
    hole, particle = exchange_plain(amplitudes, ladder, cholesky)
    if n_aux > 1:
        hole = lax.dynamic_slice_in_dim(hole, aux_index * half_width, half_width, 2)
        particle = lax.psum_scatter(particle, "aux", scatter_dimension=2, tiled=True)
    orbitals = jnp.arange(NO, dtype=jnp.int32)
    first_hot = (pair_ids // NO)[:, None] == orbitals[None, :]
    second_hot = (pair_ids % NO)[:, None] == orbitals[None, :]
    hot = first_hot.astype(jnp.float32) + second_hot.astype(jnp.float32)
    occ_sum = jnp.sum(hot * occ_energy[None, :], axis=1)
    vir_cols = lax.dynamic_slice_in_dim(vir_energy, aux_index * half_width, half_width, 0)
    denominator = vir_energy[None, :, None] + vir_cols[None, None, :] - occ_sum[:, None, None]
    return (hole.astype(jnp.float32) + particle) / denominator


def solution(mesh):
    in_specs = (P(None, "pair", None), P(), P("aux", None, None), P("pair"), P(), P())
    out_specs = P("pair", None, "aux")
    return jax.shard_map(shards, mesh=mesh, in_specs=in_specs, out_specs=out_specs, check_vma=False)
```
